256 devices in a mesh: wide: 64 (over z, x, core), narrow: 4 (over y).
Axes of the slice: x: 4, y: 4, z: 8, core: 2. Of those that a mesh axis runs over, the one named last changes fastest.
Arguments:
- coeffs: bfloat16 [2, 1024, 1024, 512], P(None, 'wide', None, 'narrow'), may hold values from -3 to 3
- legendre: bfloat16 [1024, 64, 1024], P('wide'), may hold values from -3 to 3
- order_table: int32 [1024], replicated, may hold values from 0 to 1023, each once
- thresholds: float32 [512], replicated, may hold values from 0.2 to 2
Outputs:
- lowrank: float32 [64, 2048, 512], P('wide', 'narrow')
- sparse: float32 [64, 2048, 512], P('wide', 'narrow')
The draws below stay inside these ranges and needn't reach their ends.
Inputs may be any that keep to these rules, and one draw needn't show every extreme that they name: `order_table`: each order 0 to 1023 stands in exactly one slot.
All inputs are finite; a program needn't handle non-finite values.
Results may differ from the reference program's by a relative error of at most 0.0003.
Values sent between devices are 32-bit elements; how exact they have to be, the bound alone decides.
A program may use at most 128 MiB of HBM per device.

```python
import math
import jax
import jax.numpy as jnp
from jax import lax

L = 1024
NCH = 512
NPIX = 2048
ITERS = 2
CYCLES = 64


def draw_coeffs(key, part):
    key_noise, key_common, key_scale = jax.random.split(key, 3)
    noise = jnp.clip(jax.random.normal(key_noise, (2, L, L, NCH), jnp.float32), -6.0, 6.0)
    common = 0.5 * jnp.clip(jax.random.normal(key_common, (2, L, L, 1), jnp.float32), -6.0, 6.0)
    scales = jnp.exp(jax.random.uniform(key_scale, (NCH,), jnp.float32, math.log(0.3), math.log(3.0)))
    mixed = noise + 0.7 * jnp.roll(noise, 1, axis=3) + common
    return (mixed * scales * (0.5 / math.sqrt(L))).astype(jnp.bfloat16)


def draw_legendre(key, part):
    key_values, key_cycles = jax.random.split(key, 2)
    values = jnp.clip(jax.random.normal(key_values, (L, CYCLES, L), jnp.float32), -6.0, 6.0)
    cycle_scale = jnp.exp(jax.random.uniform(key_cycles, (CYCLES,), jnp.float32, math.log(0.3), math.log(3.0)))
    return (values * cycle_scale[None, :, None] / math.sqrt(L)).astype(jnp.bfloat16)


def setup_inputs(seed: int = 0) -> dict:
    keys = jax.random.split(jax.random.key(seed), 5)
    coeffs = draw_coeffs(jax.random.fold_in(keys[4], 71), 0)
    legendre = draw_legendre(jax.random.fold_in(keys[4], 71), 0)
    order_table = jax.random.permutation(keys[2], L).astype(jnp.int32)
    thresholds = jnp.clip(jnp.exp(jax.random.uniform(keys[3], (NCH,), jnp.float32, math.log(0.2), math.log(2.0))), 0.2, 2.0)
    return {"coeffs": coeffs, "legendre": legendre, "order_table": order_table, "thresholds": thresholds}


def soft_shrink(values, limits):
    return jnp.sign(values) * jnp.maximum(jnp.abs(values) - limits, 0.0)

def wiener_filter(covariance):
    chan_total = covariance.shape[0]
    ridge_shift = jnp.trace(covariance) / chan_total
    factor = jnp.linalg.cholesky(covariance + ridge_shift * jnp.eye(chan_total, dtype=covariance.dtype))
    return jax.scipy.linalg.cho_solve((factor, True), covariance)

def reference(coeffs, legendre, order_table, thresholds):
    degree_index = jnp.arange(L, dtype=jnp.int32)

    def one_slot(slot_index):
        table_slot = lax.dynamic_index_in_dim(legendre, slot_index, 0, keepdims=False)
        coeff_slot = lax.dynamic_index_in_dim(coeffs, slot_index, 1, keepdims=False)
        order_value = lax.dynamic_index_in_dim(order_table, slot_index, 0, keepdims=False)
        degree_mask = (degree_index >= order_value).astype(legendre.dtype)
        masked_table = (table_slot * degree_mask[None, :]).astype(jnp.float32)
        return jnp.einsum('rl,klc->krc', masked_table, coeff_slot.astype(jnp.float32), precision=lax.Precision.HIGHEST)
    spectra = lax.map(one_slot, jnp.arange(L, dtype=jnp.int32))
    real_part = jnp.transpose(spectra[:, 0], (1, 2, 0))
    imag_part = jnp.transpose(spectra[:, 1], (1, 2, 0)) * (order_table != 0).astype(jnp.float32)
    bins = NPIX // 2 + 1
    real_bins = jnp.zeros((CYCLES, NCH, bins), jnp.float32).at[:, :, order_table].set(real_part)
    imag_bins = jnp.zeros((CYCLES, NCH, bins), jnp.float32).at[:, :, order_table].set(imag_part)
    sky_map = jnp.fft.irfft(lax.complex(real_bins, imag_bins), n=NPIX, axis=-1) * NPIX
    sky_field = jnp.transpose(sky_map, (0, 2, 1)).reshape(CYCLES * NPIX, NCH).astype(jnp.float32)
    lowrank = jnp.zeros_like(sky_field)
    sparse = jnp.zeros_like(sky_field)
    for iteration in range(ITERS):
        sparse = soft_shrink(sky_field - lowrank, thresholds)
        residue = sky_field - sparse
        covariance = jnp.dot(residue.T.astype(jnp.float32), residue.astype(jnp.float32), precision=lax.Precision.HIGHEST, preferred_element_type=jnp.float32)
        lowrank = jnp.dot(residue.astype(jnp.float32), wiener_filter(covariance).astype(jnp.float32), precision=lax.Precision.HIGHEST, preferred_element_type=jnp.float32)
    return (lowrank.reshape(CYCLES, NPIX, NCH), sparse.reshape(CYCLES, NPIX, NCH))
```

```python
import functools
import math

import jax
import jax.numpy as jnp
from jax import lax
from jax.experimental import pallas as pl
from jax.experimental.pallas import tpu as pltpu
from jax.sharding import PartitionSpec as P

MESH = pl.DeviceIdType.MESH
F32 = jnp.float32
BF16 = jnp.bfloat16

NPIX = 2048
NCH = 512
NB = 4
PAIRS = [(i, j) for i in range(NB) for j in range(i, NB)]
ROWS = 128 * len(PAIRS)
HALF = ROWS // 2
X, Y, Z = 4, 4, 8
CHUNK = HALF // (X * Y)
LIMIT = 64 * 1024 * 1024 - 65536 - 8192

KAPPA = NCH + 1.0
OMEGA = 2.0 / (KAPPA + 1.0)


def newton_scales():
    delta = (KAPPA - 1.0) / (KAPPA + 1.0)
    scales = []
    while delta > 1e-4:
        scales.append(2.0 / (2.0 - delta * delta))
        delta = delta * delta / (2.0 - delta * delta)
    return scales


SCALES = newton_scales()


def split(x):
    hi = x.astype(BF16)
    return hi, (x - hi.astype(F32)).astype(BF16)


def dot(a, b):
    return jnp.dot(a, b, preferred_element_type=F32)


def put_left(ref, x):
    n = x.shape[1]
    hi, lo = split(x)
    ref[:, 0:n] = hi
    ref[:, n : 2 * n] = lo
    ref[:, 2 * n : 3 * n] = hi


def put_right(ref, x):
    n = x.shape[0]
    hi, lo = split(x)
    ref[0:n, :] = hi
    ref[n : 2 * n, :] = hi
    ref[2 * n : 3 * n, :] = lo


def reduce_kernel(p_ref, out_ref, b1, acc1, b2, acc2, b3, acc3, s1, r1, s2, r2, s3, r3, s4, r4, s5, r5):
    w = lax.axis_index("wide")
    y = lax.axis_index("narrow")
    core = lax.rem(w, 2)
    x = lax.rem(w // 2, X)
    z = w // (2 * X)
    other = 1 - core
    partner = (w + 1 - 2 * core, y)

    def plane(k):
        dx, dy = k // Y, k % Y
        px, py = lax.rem(x + dx, X), lax.rem(y + dy, Y)
        return (z * 2 * X + px * 2 + core, py), px * Y + py

    def deep(d):
        return (lax.rem(z + d, Z) * 2 * X + x * 2 + core, y)

    barrier = pltpu.get_barrier_semaphore()
    peers = [partner] + [plane(k)[0] for k in range(1, X * Y)] + [deep(d) for d in range(1, Z)]
    for peer in peers:
        pl.semaphore_signal(barrier, inc=1, device_id=peer, device_id_type=MESH)
    pl.semaphore_wait(barrier, len(peers))

    order = sorted(range(X * Y), key=lambda k: -(min(k // Y, X - k // Y) + min(k % Y, Y - k % Y)))

    def rows(side, g):
        return pl.ds(pl.multiple_of(side * HALF + g * CHUNK, 8), CHUNK)

    def remote(src, dst, send, recv, peer):
        return pltpu.make_async_remote_copy(
            src_ref=src, dst_ref=dst, send_sem=send, recv_sem=recv, device_id=peer, device_id_type=MESH
        )

    first, second = {}, {}
    for k in order:
        first[k] = remote(p_ref.at[rows(other, plane(k)[1])], b1.at[k], s1.at[k], r1.at[k], partner)
        first[k].start()
    for k in order:
        peer, g = plane(k)
        first[k].wait_recv()
        acc1[k] = p_ref[rows(core, g)] + b1[k]
        if k:
            second[k] = remote(acc1.at[k], b2.at[k], s2.at[k], r2.at[k], peer)
            second[k].start()
    total = acc1[0]
    for k in order:
        if k:
            second[k].wait_recv()
            total = total + b2[k]
    acc2[...] = total
    third = {}
    for d in (4, 3, 5, 2, 6, 1, 7):
        third[d] = remote(acc2, b3.at[d], s3.at[d], r3.at[d], deep(d))
        third[d].start()
    total = acc2[...]
    for d in (1, 7, 2, 6, 3, 5, 4):
        third[d].wait_recv()
        total = total + b3[d]
    acc3[...] = total
    mine = rows(core, x * Y + y)
    fourth, fifth = {}, {}
    for k in order:
        if k:
            fourth[k] = remote(acc3, out_ref.at[mine], s4.at[k], r4.at[k], plane(k)[0])
            fourth[k].start()
    fifth[0] = remote(acc3, out_ref.at[mine], s5.at[0], r5.at[0], partner)
    fifth[0].start()
    out_ref[mine] = total
    for k in reversed(order):
        if k:
            px, py = lax.rem(x + X - k // Y, X), lax.rem(y + Y - k % Y, Y)
            got = rows(core, px * Y + py)
            fourth[k].wait_recv()
            fifth[k] = remote(out_ref.at[got], out_ref.at[got], s5.at[k], r5.at[k], partner)
            fifth[k].start()
    for k in order:
        fifth[k].wait_recv()
    for k in order:
        first[k].wait_send()
        fifth[k].wait_send()
        if k:
            second[k].wait_send()
            fourth[k].wait_send()
    for d in range(1, Z):
        third[d].wait_send()


def reduce_packed(packed):
    n = X * Y
    dma = pltpu.SemaphoreType.DMA
    return pl.pallas_call(
        reduce_kernel,
        name="reduce_packed",
        out_shape=jax.ShapeDtypeStruct((ROWS, 128), F32),
        in_specs=[pl.BlockSpec(memory_space=pltpu.VMEM)],
        out_specs=pl.BlockSpec(memory_space=pltpu.VMEM),
        scratch_shapes=[
            pltpu.VMEM((n, CHUNK, 128), F32),
            pltpu.VMEM((n, CHUNK, 128), F32),
            pltpu.VMEM((n, CHUNK, 128), F32),
            pltpu.VMEM((CHUNK, 128), F32),
            pltpu.VMEM((Z, CHUNK, 128), F32),
            pltpu.VMEM((CHUNK, 128), F32),
        ]
        + [dma((n,))] * 4
        + [dma((Z,))] * 2
        + [dma((n,))] * 4,
        compiler_params=pltpu.CompilerParams(collective_id=0, has_side_effects=True),
    )(packed)


def put_cov(res, cov_ref, left, right):
    put_right(left, res)
    n = res.shape[0]
    right[0:n, :] = left[0:n, :]
    right[n : 2 * n, :] = left[2 * n : 3 * n, :]
    right[2 * n : 3 * n, :] = left[0:n, :]
    at = 0
    for i in range(NB):
        width = (NB - i) * 128
        rows = lax.dot_general(
            left[:, i * 128 : (i + 1) * 128],
            right[:, i * 128 :],
            (((0,), (0,)), ((), ())),
            preferred_element_type=F32,
        )
        for b in range(NB - i):
            cov_ref[at : at + 128, :] = rows[:, b * 128 : (b + 1) * 128]
            at += 128


def first_kernel(sky_ref, thr_ref, res_ref, cov_ref, left, right):
    thr = thr_ref[...]
    sky = sky_ref[...]
    res = sky - (sky - jnp.minimum(jnp.maximum(sky, -thr), thr))
    res_ref[...] = res
    put_cov(res, cov_ref, left, right)


def put_inverse(cov_ref, scales_ref, a_ref, x_ref, a3, xl, xr):
    eye = (lax.broadcasted_iota(jnp.int32, (128, 128), 0) == lax.broadcasted_iota(jnp.int32, (128, 128), 1)).astype(F32)
    diag = jnp.zeros((128, 128), F32)
    for idx, (i, j) in enumerate(PAIRS):
        if i == j:
            diag = diag + cov_ref[idx * 128 : (idx + 1) * 128, :] * eye
    total = jnp.sum(jnp.sum(diag, axis=0, keepdims=True), axis=1, keepdims=True)
    inv_t = float(NCH) / total
    for idx, (i, j) in enumerate(PAIRS):
        block = cov_ref[idx * 128 : (idx + 1) * 128, :] * inv_t
        if i == j:
            block = block + eye
            a_ref[i * 128 : (i + 1) * 128, i * 128 : (i + 1) * 128] = block
        else:
            a_ref[i * 128 : (i + 1) * 128, j * 128 : (j + 1) * 128] = block
            a_ref[j * 128 : (j + 1) * 128, i * 128 : (i + 1) * 128] = block.T
    a = a_ref[...]
    put_right(a3, a)
    full_eye = (
        lax.broadcasted_iota(jnp.int32, (NCH, NCH), 0) == lax.broadcasted_iota(jnp.int32, (NCH, NCH), 1)
    ).astype(F32)
    x = (SCALES[0] * OMEGA) * (2.0 * full_eye - OMEGA * a)
    x_ref[...] = x
    put_left(xl, x)
    put_right(xr, x)

    def step(k, carry):
        wa = dot(xl[...], a3[...])
        put_left(xl, wa)
        x = scales_ref[k] * (2.0 * x_ref[...] - dot(xl[...], xr[...]))
        x_ref[...] = x
        put_left(xl, x)
        put_right(xr, x)
        return carry

    lax.fori_loop(1, len(SCALES), step, 0)
    x = x_ref[...]
    rest = full_eye - jnp.dot(x, a_ref[...], preferred_element_type=F32, precision=lax.Precision.HIGHEST)
    x = x + dot(rest.astype(BF16), xr[0:NCH, :])
    x_ref[...] = x
    put_right(xr, x)


def low_of(res_ref, xl, xr):
    res = res_ref[...]
    put_left(xl, res)
    return res - dot(xl[...], xr[...])


def middle_kernel(scales_ref, cov_ref, res_ref, sky_ref, thr_ref, sparse_ref, res2_ref, cov2_ref, a_ref, x_ref, a3, xl, xr):
    put_inverse(cov_ref, scales_ref, a_ref, x_ref, a3, xl, xr)
    thr = thr_ref[...]
    sky = sky_ref[...]
    v = sky - low_of(res_ref, xl, xr)
    sparse = v - jnp.minimum(jnp.maximum(v, -thr), thr)
    sparse_ref[...] = sparse
    res = sky - sparse
    res2_ref[...] = res
    put_cov(res, cov2_ref, a3, xr)


def last_kernel(scales_ref, cov_ref, res_ref, low_ref, a_ref, x_ref, a3, xl, xr):
    put_inverse(cov_ref, scales_ref, a_ref, x_ref, a3, xl, xr)
    low_ref[...] = low_of(res_ref, xl, xr)


VM = pl.BlockSpec(memory_space=pltpu.VMEM)
SM = pl.BlockSpec(memory_space=pltpu.SMEM)


def inverse_scratch():
    return [
        pltpu.VMEM((NCH, NCH), F32),
        pltpu.VMEM((NCH, NCH), F32),
        pltpu.VMEM((3 * NCH, NCH), BF16),
        pltpu.VMEM((NCH, 3 * NCH), BF16),
        pltpu.VMEM((3 * NCH, NCH), BF16),
    ]


def first_stage(sky, thr):
    pix = sky.shape[0]
    return pl.pallas_call(
        first_kernel,
        name="first_stage",
        out_shape=(jax.ShapeDtypeStruct((pix, NCH), F32), jax.ShapeDtypeStruct((ROWS, 128), F32)),
        in_specs=[VM, VM],
        out_specs=(VM, VM),
        scratch_shapes=[pltpu.VMEM((3 * pix, NCH), BF16), pltpu.VMEM((3 * pix, NCH), BF16)],
    )(sky, thr)


def middle_stage(scales, cov, res, sky, thr):
    pix = sky.shape[0]
    return pl.pallas_call(
        middle_kernel,
        name="middle_stage",
        out_shape=(
            jax.ShapeDtypeStruct((pix, NCH), F32),
            jax.ShapeDtypeStruct((pix, NCH), F32),
            jax.ShapeDtypeStruct((ROWS, 128), F32),
        ),
        in_specs=[SM, VM, VM, VM, VM],
        out_specs=(VM, VM, VM),
        scratch_shapes=inverse_scratch(),
    )(scales, cov, res, sky, thr)


def last_stage(scales, cov, res):
    return pl.pallas_call(
        last_kernel,
        name="last_stage",
        out_shape=jax.ShapeDtypeStruct(res.shape, F32),
        in_specs=[SM, VM, VM],
        out_specs=VM,
        scratch_shapes=inverse_scratch(),
    )(scales, cov, res)


SB = 64
HP = NPIX // 2
STEP = 4


def pixel_kernel(spec_ref, par_ref, coarse_ref, fine_ref, sky_ref, rhs):
    ns = spec_ref.shape[1]
    even = par_ref[...]
    for k in range(2):
        value = spec_ref[k]
        for p, part in enumerate((value * even, value * (1.0 - even))):
            hi, lo = split(part)
            rhs[k * ns : (k + 1) * ns, p * 128 : (p + 1) * 128] = hi
            rhs[k * ns : (k + 1) * ns, 256 + p * 128 : 256 + (p + 1) * 128] = lo

    def step(i, carry):
        tops = []
        for q in range(STEP):
            a = i * STEP + q
            ca = coarse_ref[0, pl.ds(a, 1), :]
            sa = coarse_ref[1, pl.ds(a, 1), :]
            cb, sb = fine_ref[0], fine_ref[1]
            tops.append(jnp.concatenate([ca * cb - sa * sb, -(sa * cb + ca * sb)], axis=1))
        table = jnp.concatenate(tops, axis=0)
        hi, lo = split(table)
        top = dot(hi, rhs[...])
        low = dot(lo, rhs[:, 0:256])
        e = top[:, 0:128] + top[:, 256:384] + low[:, 0:128]
        o = top[:, 128:256] + top[:, 384:512] + low[:, 128:256]
        j = pl.multiple_of(i * (STEP * SB), STEP * SB)
        sky_ref[pl.ds(j, STEP * SB), :] = e + o
        sky_ref[pl.ds(j + HP, STEP * SB), :] = e - o
        return carry

    lax.fori_loop(0, HP // (SB * STEP), step, 0)


def pixel_stage(spec, parity, coarse, fine):
    ns = spec.shape[1]
    return pl.pallas_call(
        pixel_kernel,
        name="pixel_stage",
        out_shape=jax.ShapeDtypeStruct((NPIX, spec.shape[2]), F32),
        in_specs=[VM, VM, VM, VM],
        out_specs=VM,
        scratch_shapes=[pltpu.VMEM((2 * ns, 512), BF16)],
    )(spec, parity, coarse, fine)


def per_device(coeffs, legendre, order_table, thresholds):
    slot_count = legendre.shape[0]
    degrees = legendre.shape[2]
    first_slot = lax.axis_index("wide") * slot_count
    own_orders = lax.dynamic_slice_in_dim(order_table, first_slot, slot_count)
    degree_mask = (
        lax.broadcasted_iota(jnp.int32, (slot_count, degrees), 1) >= own_orders[:, None]
    ).astype(legendre.dtype)
    masked = legendre * degree_mask[:, None, :]
    spectra = jnp.einsum("srl,kslc->ksrc", masked, coeffs, preferred_element_type=F32)
    spec = lax.all_to_all(spectra, "wide", split_axis=2, concat_axis=1, tiled=True)[:, :, 0, :]

    weights = jnp.where(order_table == 0, 1.0, 2.0).astype(F32)[None, :]

    def small_table(steps, stride, weight):
        at = lax.broadcasted_iota(jnp.int32, (steps, 1), 0) * stride
        angle = (order_table[None, :] * at % NPIX).astype(F32) * (2.0 * math.pi / NPIX)
        return jnp.stack([weight * jnp.cos(angle), weight * jnp.sin(angle)])

    coarse = small_table(HP // SB, SB, weights)
    fine = small_table(SB, 1, 1.0)
    parity = jnp.broadcast_to((1 - order_table % 2).astype(F32)[:, None], (order_table.shape[0], 128))
    sky_map = pixel_stage(spec, parity, coarse, fine)
    sky = lax.all_to_all(sky_map, "narrow", split_axis=0, concat_axis=1, tiled=True)
    thr = thresholds[None, :]
    scales = jnp.asarray(SCALES + [0.0] * (16 - len(SCALES)), F32)
    res, cov = first_stage(sky, thr)
    sparse, res, cov = middle_stage(scales, reduce_packed(cov), res, sky, thr)
    low = last_stage(scales, reduce_packed(cov), res)
    return low[None], sparse[None]


def solution(mesh):
    placed = (P(None, "wide", None, "narrow"), P("wide", None, None), P(), P())
    return jax.shard_map(
        per_device,
        mesh=mesh,
        in_specs=placed,
        out_specs=(P("wide", "narrow", None), P("wide", "narrow", None)),
        check_vma=False,
    )
```

```python
import functools
import math

import jax
import jax.numpy as jnp
from jax import lax
from jax.experimental import pallas as pl
from jax.experimental.pallas import tpu as pltpu
from jax.sharding import PartitionSpec as P

MESH = pl.DeviceIdType.MESH
F32 = jnp.float32
BF16 = jnp.bfloat16

NPIX = 2048
NCH = 512
NB = 4
PAIRS = [(i, j) for i in range(NB) for j in range(i, NB)]
ROWS = 128 * len(PAIRS)
HALF = ROWS // 2
X, Y, Z = 4, 4, 8
CHUNK = HALF // (X * Y)
LIMIT = 64 * 1024 * 1024 - 65536 - 8192

KAPPA = NCH + 1.0
OMEGA = 2.0 / (KAPPA + 1.0)


def newton_scales():
    delta = (KAPPA - 1.0) / (KAPPA + 1.0)
    scales = []
    while delta > 1e-4:
        scales.append(2.0 / (2.0 - delta * delta))
        delta = delta * delta / (2.0 - delta * delta)
    return scales


SCALES = newton_scales()


def split(x):
    hi = x.astype(BF16)
    return hi, (x - hi.astype(F32)).astype(BF16)


def dot(a, b):
    return jnp.dot(a, b, preferred_element_type=F32)


def put_left(ref, x):
    n = x.shape[1]
    hi, lo = split(x)
    ref[:, 0:n] = hi
    ref[:, n : 2 * n] = lo
    ref[:, 2 * n : 3 * n] = hi


def put_right(ref, x):
    n = x.shape[0]
    hi, lo = split(x)
    ref[0:n, :] = hi
    ref[n : 2 * n, :] = hi
    ref[2 * n : 3 * n, :] = lo


def reduce_kernel(p_ref, out_ref, b1, acc1, b2, acc2, b3, acc3, s1, r1, s2, r2, s3, r3, s4, r4, s5, r5):
    w = lax.axis_index("wide")
    y = lax.axis_index("narrow")
    core = lax.rem(w, 2)
    x = lax.rem(w // 2, X)
    z = w // (2 * X)
    other = 1 - core
    partner = (w + 1 - 2 * core, y)

    def plane(k):
        dx, dy = k // Y, k % Y
        px, py = lax.rem(x + dx, X), lax.rem(y + dy, Y)
        return (z * 2 * X + px * 2 + core, py), px * Y + py

    def deep(d):
        return (lax.rem(z + d, Z) * 2 * X + x * 2 + core, y)

    barrier = pltpu.get_barrier_semaphore()
    peers = [partner] + [plane(k)[0] for k in range(1, X * Y)] + [deep(d) for d in range(1, Z)]
    for peer in peers:
        pl.semaphore_signal(barrier, inc=1, device_id=peer, device_id_type=MESH)
    pl.semaphore_wait(barrier, len(peers))

    order = sorted(range(X * Y), key=lambda k: -(min(k // Y, X - k // Y) + min(k % Y, Y - k % Y)))

    def rows(side, g):
        return pl.ds(pl.multiple_of(side * HALF + g * CHUNK, 8), CHUNK)

    def remote(src, dst, send, recv, peer):
        return pltpu.make_async_remote_copy(
            src_ref=src, dst_ref=dst, send_sem=send, recv_sem=recv, device_id=peer, device_id_type=MESH
        )

    first, second = {}, {}
    for k in order:
        first[k] = remote(p_ref.at[rows(other, plane(k)[1])], b1.at[k], s1.at[k], r1.at[k], partner)
        first[k].start()
    for k in order:
        peer, g = plane(k)
        first[k].wait_recv()
        acc1[k] = p_ref[rows(core, g)] + b1[k]
        if k:
            second[k] = remote(acc1.at[k], b2.at[k], s2.at[k], r2.at[k], peer)
            second[k].start()
    total = acc1[0]
    for k in order:
        if k:
            second[k].wait_recv()
            total = total + b2[k]
    acc2[...] = total
    third = {}
    for d in (4, 3, 5, 2, 6, 1, 7):
        third[d] = remote(acc2, b3.at[d], s3.at[d], r3.at[d], deep(d))
        third[d].start()
    total = acc2[...]
    for d in (1, 7, 2, 6, 3, 5, 4):
        third[d].wait_recv()
        total = total + b3[d]
    acc3[...] = total
    mine = rows(core, x * Y + y)
    fourth, fifth = {}, {}
    for k in order:
        if k:
            fourth[k] = remote(acc3, out_ref.at[mine], s4.at[k], r4.at[k], plane(k)[0])
            fourth[k].start()
    fifth[0] = remote(acc3, out_ref.at[mine], s5.at[0], r5.at[0], partner)
    fifth[0].start()
    out_ref[mine] = total
    for k in reversed(order):
        if k:
            px, py = lax.rem(x + X - k // Y, X), lax.rem(y + Y - k % Y, Y)
            got = rows(core, px * Y + py)
            fourth[k].wait_recv()
            fifth[k] = remote(out_ref.at[got], out_ref.at[got], s5.at[k], r5.at[k], partner)
            fifth[k].start()
    for k in order:
        fifth[k].wait_recv()
    for k in order:
        first[k].wait_send()
        fifth[k].wait_send()
        if k:
            second[k].wait_send()
            fourth[k].wait_send()
    for d in range(1, Z):
        third[d].wait_send()


def reduce_packed(packed):
    n = X * Y
    dma = pltpu.SemaphoreType.DMA
    return pl.pallas_call(
        reduce_kernel,
        name="reduce_packed",
        out_shape=jax.ShapeDtypeStruct((ROWS, 128), F32),
        in_specs=[pl.BlockSpec(memory_space=pltpu.VMEM)],
        out_specs=pl.BlockSpec(memory_space=pltpu.VMEM),
        scratch_shapes=[
            pltpu.VMEM((n, CHUNK, 128), F32),
            pltpu.VMEM((n, CHUNK, 128), F32),
            pltpu.VMEM((n, CHUNK, 128), F32),
            pltpu.VMEM((CHUNK, 128), F32),
            pltpu.VMEM((Z, CHUNK, 128), F32),
            pltpu.VMEM((CHUNK, 128), F32),
        ]
        + [dma((n,))] * 4
        + [dma((Z,))] * 2
        + [dma((n,))] * 4,
        compiler_params=pltpu.CompilerParams(collective_id=0, has_side_effects=True),
    )(packed)


def put_cov(res, cov_ref, left, right):
    put_right(left, res)
    n = res.shape[0]
    right[0:n, :] = left[0:n, :]
    right[n : 2 * n, :] = left[2 * n : 3 * n, :]
    right[2 * n : 3 * n, :] = left[0:n, :]
    at = 0
    for i in range(NB):
        width = (NB - i) * 128
        rows = lax.dot_general(
            left[:, i * 128 : (i + 1) * 128],
            right[:, i * 128 :],
            (((0,), (0,)), ((), ())),
            preferred_element_type=F32,
        )
        for b in range(NB - i):
            cov_ref[at : at + 128, :] = rows[:, b * 128 : (b + 1) * 128]
            at += 128


def first_kernel(parts_ref, thr_ref, sky_ref, res_ref, cov_ref, left, right):
    thr = thr_ref[...]
    sky = jnp.concatenate([parts_ref[i] for i in range(NB)], axis=1)
    sky_ref[...] = sky
    res = sky - (sky - jnp.minimum(jnp.maximum(sky, -thr), thr))
    res_ref[...] = res
    put_cov(res, cov_ref, left, right)


def put_inverse(cov_ref, scales_ref, a_ref, x_ref, a3, xl, xr):
    eye = (lax.broadcasted_iota(jnp.int32, (128, 128), 0) == lax.broadcasted_iota(jnp.int32, (128, 128), 1)).astype(F32)
    diag = jnp.zeros((128, 128), F32)
    for idx, (i, j) in enumerate(PAIRS):
        if i == j:
            diag = diag + cov_ref[idx * 128 : (idx + 1) * 128, :] * eye
    total = jnp.sum(jnp.sum(diag, axis=0, keepdims=True), axis=1, keepdims=True)
    inv_t = float(NCH) / total
    for idx, (i, j) in enumerate(PAIRS):
        block = cov_ref[idx * 128 : (idx + 1) * 128, :] * inv_t
        if i == j:
            block = block + eye
            a_ref[i * 128 : (i + 1) * 128, i * 128 : (i + 1) * 128] = block
        else:
            a_ref[i * 128 : (i + 1) * 128, j * 128 : (j + 1) * 128] = block
            a_ref[j * 128 : (j + 1) * 128, i * 128 : (i + 1) * 128] = block.T
    a = a_ref[...]
    put_right(a3, a)
    full_eye = (
        lax.broadcasted_iota(jnp.int32, (NCH, NCH), 0) == lax.broadcasted_iota(jnp.int32, (NCH, NCH), 1)
    ).astype(F32)
    x = (SCALES[0] * OMEGA) * (2.0 * full_eye - OMEGA * a)
    x_ref[...] = x
    put_left(xl, x)
    put_right(xr, x)

    def step(k, carry):
        wa = dot(xl[...], a3[...])
        put_left(xl, wa)
        x = scales_ref[k] * (2.0 * x_ref[...] - dot(xl[...], xr[...]))
        x_ref[...] = x
        put_left(xl, x)
        put_right(xr, x)
        return carry

    lax.fori_loop(1, len(SCALES), step, 0)
    x = x_ref[...]
    rest = full_eye - jnp.dot(x, a_ref[...], preferred_element_type=F32, precision=lax.Precision.HIGHEST)
    x = x + dot(rest.astype(BF16), xr[0:NCH, :])
    x_ref[...] = x
    put_right(xr, x)


def low_of(res_ref, xl, xr):
    res = res_ref[...]
    put_left(xl, res)
    return res - dot(xl[...], xr[...])


def middle_kernel(scales_ref, cov_ref, res_ref, sky_ref, thr_ref, sparse_ref, res2_ref, cov2_ref, a_ref, x_ref, a3, xl, xr):
    put_inverse(cov_ref, scales_ref, a_ref, x_ref, a3, xl, xr)
    thr = thr_ref[...]
    sky = sky_ref[...]
    v = sky - low_of(res_ref, xl, xr)
    sparse = v - jnp.minimum(jnp.maximum(v, -thr), thr)
    sparse_ref[...] = sparse
    res = sky - sparse
    res2_ref[...] = res
    put_cov(res, cov2_ref, a3, xr)


def last_kernel(scales_ref, cov_ref, res_ref, low_ref, a_ref, x_ref, a3, xl, xr):
    put_inverse(cov_ref, scales_ref, a_ref, x_ref, a3, xl, xr)
    low_ref[...] = low_of(res_ref, xl, xr)


VM = pl.BlockSpec(memory_space=pltpu.VMEM)
SM = pl.BlockSpec(memory_space=pltpu.SMEM)


def inverse_scratch():
    return [
        pltpu.VMEM((NCH, NCH), F32),
        pltpu.VMEM((NCH, NCH), F32),
        pltpu.VMEM((3 * NCH, NCH), BF16),
        pltpu.VMEM((NCH, 3 * NCH), BF16),
        pltpu.VMEM((3 * NCH, NCH), BF16),
    ]


def first_stage(parts, thr):
    pix = parts.shape[1]
    return pl.pallas_call(
        first_kernel,
        name="first_stage",
        out_shape=(
            jax.ShapeDtypeStruct((pix, NCH), F32),
            jax.ShapeDtypeStruct((pix, NCH), F32),
            jax.ShapeDtypeStruct((ROWS, 128), F32),
        ),
        in_specs=[VM, VM],
        out_specs=(VM, VM, VM),
        scratch_shapes=[pltpu.VMEM((3 * pix, NCH), BF16), pltpu.VMEM((3 * pix, NCH), BF16)],
    )(parts, thr)


def middle_stage(scales, cov, res, sky, thr):
    pix = sky.shape[0]
    return pl.pallas_call(
        middle_kernel,
        name="middle_stage",
        out_shape=(
            jax.ShapeDtypeStruct((pix, NCH), F32),
            jax.ShapeDtypeStruct((pix, NCH), F32),
            jax.ShapeDtypeStruct((ROWS, 128), F32),
        ),
        in_specs=[SM, VM, VM, VM, VM],
        out_specs=(VM, VM, VM),
        scratch_shapes=inverse_scratch(),
    )(scales, cov, res, sky, thr)


def last_stage(scales, cov, res):
    return pl.pallas_call(
        last_kernel,
        name="last_stage",
        out_shape=jax.ShapeDtypeStruct(res.shape, F32),
        in_specs=[SM, VM, VM],
        out_specs=VM,
        scratch_shapes=inverse_scratch(),
    )(scales, cov, res)


SB = 64
HP = NPIX // 2
WIDE = 2 * X * Z
GROUPS = 2
SUBS = 2


def front_kernel(
    ord_ref, row_ref, leg_hbm, co_hbm, out_ref,
    leg_v, co_v, sp, rb, th, tl, trig_a, trig_b, par, rhs, stage,
    ls, s1, r1, s2, r2,
):
    slots, cycles, degrees = leg_v.shape
    total = WIDE * slots
    gs = slots // GROUPS
    w = lax.axis_index("wide")
    y = lax.axis_index("narrow")
    core = lax.rem(w, 2)
    x = lax.rem(w // 2, X)
    z = w // (2 * X)

    offsets = [(dz, dx, dc) for dz in range(Z) for dx in range(X) for dc in range(2)][1:]
    offsets.sort(key=lambda o: (-min(o[0], Z - o[0]) - min(o[1], X - o[1]), o[1], o[2], o[0]))

    def at(sign, o):
        dz, dx, dc = o
        pz = lax.rem(z + (dz if sign > 0 else Z - dz), Z)
        px = lax.rem(x + (dx if sign > 0 else X - dx), X)
        return pz * 2 * X + px * 2 + (lax.rem(core + dc, 2))

    def ring(d):
        return (w, lax.rem(y + d, Y))

    def loads(s):
        return [pltpu.make_async_copy(leg_hbm.at[s], leg_v.at[s], ls.at[0, s])] + [
            pltpu.make_async_copy(co_hbm.at[k, s], co_v.at[s, :, k * 128 : (k + 1) * 128], ls.at[1 + k, s])
            for k in range(2)
        ]

    pending = [loads(s) for s in range(slots)]
    for copies in pending:
        for copy in copies:
            copy.start()

    barrier = pltpu.get_barrier_semaphore()
    for o in offsets:
        pl.semaphore_signal(barrier, inc=1, device_id=(at(1, o), y), device_id_type=MESH)
    for d in range(1, Y):
        pl.semaphore_signal(barrier, inc=1, device_id=ring(d), device_id_type=MESH)

    def remote(src, dst, send, recv, peer):
        return pltpu.make_async_remote_copy(
            src_ref=src, dst_ref=dst, send_sem=send, recv_sem=recv, device_id=peer, device_id_type=MESH
        )

    degree = lax.broadcasted_iota(jnp.int32, (cycles, degrees), 1)
    sends = {}
    for g in range(GROUPS):
        for t in range(gs):
            s = g * gs + t
            for copy in pending[s]:
                copy.wait()
            order = ord_ref[w * slots + s]
            table = jnp.where(degree >= order, leg_v[s].astype(F32), 0.0).astype(BF16)
            value = dot(table, co_v[s])
            for k in range(2):
                sp[g, pl.ds(k * gs + t, cycles, stride=2 * gs), :] = value[:, k * 128 : (k + 1) * 128]
        if g == 0:
            pl.semaphore_wait(barrier, len(offsets) + Y - 1)
        for r, o in enumerate(offsets):
            to = at(1, o)
            sends[g, r] = remote(
                sp.at[g, pl.ds(pl.multiple_of(to * 2 * gs, 8), 2 * gs), :], rb.at[g, w], s1.at[g, r], r1.at[g, r], (to, y)
            )
            sends[g, r].start()

    orders = row_ref[...]
    weights = jnp.where(orders == 0, 1.0, 2.0).astype(F32)

    def trig(ref, steps, stride, weight):
        turn = orders * (lax.broadcasted_iota(jnp.int32, (steps, total), 0) * stride)
        angle = jnp.bitwise_and(turn, NPIX - 1).astype(F32) * (2.0 * math.pi / NPIX)
        ref[0] = weight * jnp.cos(angle)
        ref[1] = weight * jnp.sin(angle)

    trig(trig_a, HP // SB, SB, weights)
    trig(trig_b, SB, 1, 1.0)
    even = (1 - jnp.bitwise_and(orders, 1)).astype(F32)
    for b in range(total // 128):
        par[b * 128 : (b + 1) * 128, :] = jnp.broadcast_to(even[:, b * 128 : (b + 1) * 128], (128, 128)).T

    def fill(a, carry):
        rows = pl.ds(pl.multiple_of(a * SB, SB), SB)
        ca = trig_a[0, pl.ds(a, 1), :]
        sa = trig_a[1, pl.ds(a, 1), :]
        cb, sb = trig_b[0], trig_b[1]
        for k, value in enumerate((ca * cb - sa * sb, -(sa * cb + ca * sb))):
            hi, lo = split(value)
            th[rows, k * total : (k + 1) * total] = hi
            tl[rows, k * total : (k + 1) * total] = lo
        return carry

    lax.fori_loop(0, HP // SB, fill, 0)

    def prepare(src):
        rows = pl.ds(pl.multiple_of(src * slots, slots), slots)
        evens = par[rows, :]
        for k in range(2):
            value = jnp.concatenate([rb[g, src, k * gs : (k + 1) * gs, :] for g in range(GROUPS)], axis=0)
            own = value * evens
            at_k = pl.ds(pl.multiple_of(k * total + src * slots, slots), slots)
            for p, part in enumerate((own, value - own)):
                hi, lo = split(part)
                rhs[at_k, p * 128 : (p + 1) * 128] = hi
                rhs[at_k, 256 + p * 128 : 256 + (p + 1) * 128] = lo

    for g in range(GROUPS):
        rb[g, w] = sp[g, pl.ds(pl.multiple_of(w * 2 * gs, 8), 2 * gs), :]
    prepare(w)
    for r, o in enumerate(offsets):
        for g in range(GROUPS):
            sends[g, r].wait_recv()
        prepare(at(-1, o))

    width = NPIX // Y
    sub = width // SUBS
    outs = {}
    for d in (2, 1):
        first = lax.rem(y + d, Y)
        sign = jnp.where(first < Y // 2, 1.0, -1.0).astype(F32)
        start = lax.rem(first, Y // 2) * width
        for b in range(SUBS):
            rows = pl.ds(pl.multiple_of(start + b * sub, sub), sub)
            top = dot(th[rows, :], rhs[...])
            low = dot(tl[rows, :], rhs[:, 0:256])
            e = top[:, 0:128] + top[:, 256:384] + low[:, 0:128]
            o = sign * (top[:, 128:256] + top[:, 384:512] + low[:, 128:256])
            for q, value in ((d, e + o), ((d + 2) % Y, e - o)):
                mine = slice(b * sub, (b + 1) * sub)
                if q == 0:
                    out_ref[y, mine, :] = value
                else:
                    stage[q - 1, mine, :] = value
                    outs[q, b] = remote(
                        stage.at[q - 1, mine, :], out_ref.at[y, mine, :], s2.at[q, b], r2.at[q, b], ring(q)
                    )
                    outs[q, b].start()
    for copy in outs.values():
        copy.wait_recv()
    for copy in outs.values():
        copy.wait_send()
    for copy in sends.values():
        copy.wait_send()


def front_stage(order_table, legendre, coeffs):
    slots, cycles, degrees = legendre.shape
    total = WIDE * slots
    gs = slots // GROUPS
    width = NPIX // Y
    dma = pltpu.SemaphoreType.DMA
    hbm = pl.BlockSpec(memory_space=pl.ANY)
    return pl.pallas_call(
        front_kernel,
        name="front_stage",
        out_shape=jax.ShapeDtypeStruct((Y, width, 128), F32),
        in_specs=[SM, VM, hbm, hbm],
        out_specs=VM,
        scratch_shapes=[
            pltpu.VMEM((slots, cycles, degrees), BF16),
            pltpu.VMEM((slots, degrees, 256), BF16),
            pltpu.VMEM((GROUPS, cycles * 2 * gs, 128), F32),
            pltpu.VMEM((GROUPS, WIDE, 2 * gs, 128), F32),
            pltpu.VMEM((HP, 2 * total), BF16),
            pltpu.VMEM((HP, 2 * total), BF16),
            pltpu.VMEM((2, HP // SB, total), F32),
            pltpu.VMEM((2, SB, total), F32),
            pltpu.VMEM((total, 128), F32),
            pltpu.VMEM((2 * total, 512), BF16),
            pltpu.VMEM((Y - 1, width, 128), F32),
            dma((3, slots)),
            dma((GROUPS, WIDE)),
            dma((GROUPS, WIDE)),
            dma((Y, SUBS)),
            dma((Y, SUBS)),
        ],
        compiler_params=pltpu.CompilerParams(collective_id=1, has_side_effects=True),
    )(order_table, order_table[None, :], legendre, coeffs)


def per_device(coeffs, legendre, order_table, thresholds):
    parts = front_stage(order_table, legendre, coeffs)
    thr = thresholds[None, :]
    scales = jnp.asarray(SCALES + [0.0] * (16 - len(SCALES)), F32)
    sky, res, cov = first_stage(parts, thr)
    sparse, res, cov = middle_stage(scales, reduce_packed(cov), res, sky, thr)
    low = last_stage(scales, reduce_packed(cov), res)
    return low[None], sparse[None]


def solution(mesh):
    placed = (P(None, "wide", None, "narrow"), P("wide", None, None), P(), P())
    return jax.shard_map(
        per_device,
        mesh=mesh,
        in_specs=placed,
        out_specs=(P("wide", "narrow", None), P("wide", "narrow", None)),
        check_vma=False,
    )
```

```python
import functools
import math

import jax
import jax.numpy as jnp
from jax import lax
from jax.experimental import pallas as pl
from jax.experimental.pallas import tpu as pltpu
from jax.sharding import PartitionSpec as P

MESH = pl.DeviceIdType.MESH
F32 = jnp.float32
BF16 = jnp.bfloat16

NPIX = 2048
NCH = 512
NB = 4
PAIRS = [(i, j) for i in range(NB) for j in range(i, NB)]
ROWS = 128 * len(PAIRS)
HALF = ROWS // 2
X, Y, Z = 4, 4, 8
CHUNK = HALF // (X * Y)
LIMIT = 64 * 1024 * 1024 - 65536 - 8192

KAPPA = NCH + 1.0
OMEGA = 2.0 / (KAPPA + 1.0)


def newton_scales():
    delta = (KAPPA - 1.0) / (KAPPA + 1.0)
    scales = []
    while delta > 1e-4:
        scales.append(2.0 / (2.0 - delta * delta))
        delta = delta * delta / (2.0 - delta * delta)
    return scales


SCALES = newton_scales()


def split(x):
    hi = x.astype(BF16)
    return hi, (x - hi.astype(F32)).astype(BF16)


def dot(a, b):
    return jnp.dot(a, b, preferred_element_type=F32)


def put_left(ref, x):
    n = x.shape[1]
    hi, lo = split(x)
    ref[:, 0:n] = hi
    ref[:, n : 2 * n] = lo
    ref[:, 2 * n : 3 * n] = hi


def put_right(ref, x):
    n = x.shape[0]
    hi, lo = split(x)
    ref[0:n, :] = hi
    ref[n : 2 * n, :] = hi
    ref[2 * n : 3 * n, :] = lo


def reduce_peers():
    w = lax.axis_index("wide")
    y = lax.axis_index("narrow")
    core = lax.rem(w, 2)
    x = lax.rem(w // 2, X)
    z = w // (2 * X)
    other = 1 - core
    partner = (w + 1 - 2 * core, y)

    def plane(k):
        dx, dy = k // Y, k % Y
        px, py = lax.rem(x + dx, X), lax.rem(y + dy, Y)
        return (z * 2 * X + px * 2 + core, py), px * Y + py

    def deep(d):
        return (lax.rem(z + d, Z) * 2 * X + x * 2 + core, y)

    return x, y, core, other, partner, plane, deep


def greet():
    _, _, _, _, partner, plane, deep = reduce_peers()
    barrier = pltpu.get_barrier_semaphore()
    for peer in [partner] + [plane(k)[0] for k in range(1, X * Y)] + [deep(d) for d in range(1, Z)]:
        pl.semaphore_signal(barrier, inc=1, device_id=peer, device_id_type=MESH)


def reduce_all(p_ref, out_ref, b1, acc1, b2, acc2, b3, acc3, s1, r1, s2, r2, s3, r3, s4, r4, s5, r5):
    x, y, core, other, partner, plane, deep = reduce_peers()
    pl.semaphore_wait(pltpu.get_barrier_semaphore(), X * Y + Z - 1)

    order = sorted(range(X * Y), key=lambda k: -(min(k // Y, X - k // Y) + min(k % Y, Y - k % Y)))

    def rows(side, g):
        return pl.ds(pl.multiple_of(side * HALF + g * CHUNK, 8), CHUNK)

    def remote(src, dst, send, recv, peer):
        return pltpu.make_async_remote_copy(
            src_ref=src, dst_ref=dst, send_sem=send, recv_sem=recv, device_id=peer, device_id_type=MESH
        )

    first, second = {}, {}
    for k in order:
        first[k] = remote(p_ref.at[rows(other, plane(k)[1])], b1.at[k], s1.at[k], r1.at[k], partner)
        first[k].start()
    for k in order:
        peer, g = plane(k)
        first[k].wait_recv()
        acc1[k] = p_ref[rows(core, g)] + b1[k]
        if k:
            second[k] = remote(acc1.at[k], b2.at[k], s2.at[k], r2.at[k], peer)
            second[k].start()
    total = acc1[0]
    for k in order:
        if k:
            second[k].wait_recv()
            total = total + b2[k]
    acc2[...] = total
    third = {}
    for d in (4, 3, 5, 2, 6, 1, 7):
        third[d] = remote(acc2, b3.at[d], s3.at[d], r3.at[d], deep(d))
        third[d].start()
    total = acc2[...]
    for d in (1, 7, 2, 6, 3, 5, 4):
        third[d].wait_recv()
        total = total + b3[d]
    acc3[...] = total
    mine = rows(core, x * Y + y)
    fourth, fifth = {}, {}
    for k in order:
        if k:
            fourth[k] = remote(acc3, out_ref.at[mine], s4.at[k], r4.at[k], plane(k)[0])
            fourth[k].start()
    fifth[0] = remote(acc3, out_ref.at[mine], s5.at[0], r5.at[0], partner)
    fifth[0].start()
    out_ref[mine] = total
    for k in reversed(order):
        if k:
            px, py = lax.rem(x + X - k // Y, X), lax.rem(y + Y - k % Y, Y)
            got = rows(core, px * Y + py)
            fourth[k].wait_recv()
            fifth[k] = remote(out_ref.at[got], out_ref.at[got], s5.at[k], r5.at[k], partner)
            fifth[k].start()
    for k in order:
        fifth[k].wait_recv()
    for k in order:
        first[k].wait_send()
        fifth[k].wait_send()
        if k:
            second[k].wait_send()
            fourth[k].wait_send()
    for d in range(1, Z):
        third[d].wait_send()


def reduce_scratch():
    n = X * Y
    dma = pltpu.SemaphoreType.DMA
    return (
        [
            pltpu.VMEM((ROWS, 128), F32),
            pltpu.VMEM((n, CHUNK, 128), F32),
            pltpu.VMEM((n, CHUNK, 128), F32),
            pltpu.VMEM((n, CHUNK, 128), F32),
            pltpu.VMEM((CHUNK, 128), F32),
            pltpu.VMEM((Z, CHUNK, 128), F32),
            pltpu.VMEM((CHUNK, 128), F32),
        ]
        + [dma((n,))] * 4
        + [dma((Z,))] * 2
        + [dma((n,))] * 4
    )


def put_cov(res, cov_ref, left, right):
    put_right(left, res)
    n = res.shape[0]
    right[0:n, :] = left[0:n, :]
    right[n : 2 * n, :] = left[2 * n : 3 * n, :]
    right[2 * n : 3 * n, :] = left[0:n, :]
    at = 0
    for i in range(NB):
        width = (NB - i) * 128
        rows = lax.dot_general(
            left[:, i * 128 : (i + 1) * 128],
            right[:, i * 128 :],
            (((0,), (0,)), ((), ())),
            preferred_element_type=F32,
        )
        for b in range(NB - i):
            cov_ref[at : at + 128, :] = rows[:, b * 128 : (b + 1) * 128]
            at += 128


def first_kernel(parts_ref, thr_ref, sky_ref, res_ref, cov_ref, left, right, part_ref, *reduce_refs):
    greet()
    thr = thr_ref[...]
    sky = jnp.concatenate([parts_ref[i] for i in range(NB)], axis=1)
    sky_ref[...] = sky
    res = sky - (sky - jnp.minimum(jnp.maximum(sky, -thr), thr))
    res_ref[...] = res
    put_cov(res, part_ref, left, right)
    reduce_all(part_ref, cov_ref, *reduce_refs)


def put_inverse(cov_ref, scales_ref, a_ref, x_ref, a3, xl, xr):
    eye = (lax.broadcasted_iota(jnp.int32, (128, 128), 0) == lax.broadcasted_iota(jnp.int32, (128, 128), 1)).astype(F32)
    diag = jnp.zeros((128, 128), F32)
    for idx, (i, j) in enumerate(PAIRS):
        if i == j:
            diag = diag + cov_ref[idx * 128 : (idx + 1) * 128, :] * eye
    total = jnp.sum(jnp.sum(diag, axis=0, keepdims=True), axis=1, keepdims=True)
    inv_t = float(NCH) / total
    for idx, (i, j) in enumerate(PAIRS):
        block = cov_ref[idx * 128 : (idx + 1) * 128, :] * inv_t
        if i == j:
            block = block + eye
            a_ref[i * 128 : (i + 1) * 128, i * 128 : (i + 1) * 128] = block
        else:
            a_ref[i * 128 : (i + 1) * 128, j * 128 : (j + 1) * 128] = block
            a_ref[j * 128 : (j + 1) * 128, i * 128 : (i + 1) * 128] = block.T
    a = a_ref[...]
    put_right(a3, a)
    full_eye = (
        lax.broadcasted_iota(jnp.int32, (NCH, NCH), 0) == lax.broadcasted_iota(jnp.int32, (NCH, NCH), 1)
    ).astype(F32)
    x = (SCALES[0] * OMEGA) * (2.0 * full_eye - OMEGA * a)
    x_ref[...] = x
    put_left(xl, x)
    put_right(xr, x)

    def step(k, carry):
        wa = dot(xl[...], a3[...])
        put_left(xl, wa)
        x = scales_ref[k] * (2.0 * x_ref[...] - dot(xl[...], xr[...]))
        x_ref[...] = x
        put_left(xl, x)
        put_right(xr, x)
        return carry

    lax.fori_loop(1, len(SCALES), step, 0)
    x = x_ref[...]
    rest = full_eye - jnp.dot(x, a_ref[...], preferred_element_type=F32, precision=lax.Precision.HIGHEST)
    x = x + dot(rest.astype(BF16), xr[0:NCH, :])
    x_ref[...] = x
    put_right(xr, x)


def low_of(res_ref, xl, xr):
    res = res_ref[...]
    put_left(xl, res)
    return res - dot(xl[...], xr[...])


def middle_kernel(
    scales_ref, cov_ref, res_ref, sky_ref, thr_ref, sparse_ref, res2_ref, cov2_ref,
    a_ref, x_ref, a3, xl, xr, part_ref, *reduce_refs,
):
    greet()
    put_inverse(cov_ref, scales_ref, a_ref, x_ref, a3, xl, xr)
    thr = thr_ref[...]
    sky = sky_ref[...]
    v = sky - low_of(res_ref, xl, xr)
    sparse = v - jnp.minimum(jnp.maximum(v, -thr), thr)
    sparse_ref[...] = sparse
    res = sky - sparse
    res2_ref[...] = res
    put_cov(res, part_ref, a3, xr)
    reduce_all(part_ref, cov2_ref, *reduce_refs)


def last_kernel(scales_ref, cov_ref, res_ref, sparse_ref, low_ref, out_ref, a_ref, x_ref, a3, xl, xr, sem):
    copy = pltpu.make_async_copy(sparse_ref, out_ref, sem)
    copy.start()
    put_inverse(cov_ref, scales_ref, a_ref, x_ref, a3, xl, xr)
    low_ref[...] = low_of(res_ref, xl, xr)
    copy.wait()


VM = pl.BlockSpec(memory_space=pltpu.VMEM)
SM = pl.BlockSpec(memory_space=pltpu.SMEM)


def inverse_scratch():
    return [
        pltpu.VMEM((NCH, NCH), F32),
        pltpu.VMEM((NCH, NCH), F32),
        pltpu.VMEM((3 * NCH, NCH), BF16),
        pltpu.VMEM((NCH, 3 * NCH), BF16),
        pltpu.VMEM((3 * NCH, NCH), BF16),
    ]


def first_stage(parts, thr):
    pix = parts.shape[1]
    return pl.pallas_call(
        first_kernel,
        name="first_stage",
        out_shape=(
            jax.ShapeDtypeStruct((pix, NCH), F32),
            jax.ShapeDtypeStruct((pix, NCH), F32),
            jax.ShapeDtypeStruct((ROWS, 128), F32),
        ),
        in_specs=[VM, VM],
        out_specs=(VM, VM, VM),
        scratch_shapes=[pltpu.VMEM((3 * pix, NCH), BF16), pltpu.VMEM((3 * pix, NCH), BF16)] + reduce_scratch(),
        compiler_params=pltpu.CompilerParams(collective_id=2, has_side_effects=True),
    )(parts, thr)


def middle_stage(scales, cov, res, sky, thr):
    pix = sky.shape[0]
    return pl.pallas_call(
        middle_kernel,
        name="middle_stage",
        out_shape=(
            jax.ShapeDtypeStruct((pix, NCH), F32),
            jax.ShapeDtypeStruct((pix, NCH), F32),
            jax.ShapeDtypeStruct((ROWS, 128), F32),
        ),
        in_specs=[SM, VM, VM, VM, VM],
        out_specs=(VM, VM, VM),
        scratch_shapes=inverse_scratch() + reduce_scratch(),
        compiler_params=pltpu.CompilerParams(collective_id=3, has_side_effects=True),
    )(scales, cov, res, sky, thr)


def last_stage(scales, cov, res, sparse):
    return pl.pallas_call(
        last_kernel,
        name="last_stage",
        out_shape=(jax.ShapeDtypeStruct(res.shape, F32), jax.ShapeDtypeStruct(res.shape, F32)),
        in_specs=[SM, VM, VM, VM],
        out_specs=(VM, pl.BlockSpec(memory_space=pl.ANY)),
        scratch_shapes=inverse_scratch() + [pltpu.SemaphoreType.DMA],
    )(scales, cov, res, sparse)


SB = 64
HP = NPIX // 2
WIDE = 2 * X * Z
GROUPS = 2
SUBS = 2


def front_kernel(
    ord_ref, row_ref, leg_hbm, co_hbm, out_ref,
    leg_v, co_v, sp, rb, th, tl, trig_a, trig_b, par, rhs, stage,
    ls, s1, r1, s2, r2,
):
    slots, cycles, degrees = leg_v.shape
    total = WIDE * slots
    gs = slots // GROUPS
    w = lax.axis_index("wide")
    y = lax.axis_index("narrow")
    core = lax.rem(w, 2)
    x = lax.rem(w // 2, X)
    z = w // (2 * X)

    offsets = [(dz, dx, dc) for dz in range(Z) for dx in range(X) for dc in range(2)][1:]
    offsets.sort(key=lambda o: (-min(o[0], Z - o[0]) - min(o[1], X - o[1]), o[1], o[2], o[0]))

    def at(sign, o):
        dz, dx, dc = o
        pz = lax.rem(z + (dz if sign > 0 else Z - dz), Z)
        px = lax.rem(x + (dx if sign > 0 else X - dx), X)
        return pz * 2 * X + px * 2 + (lax.rem(core + dc, 2))

    def ring(d):
        return (w, lax.rem(y + d, Y))

    def loads(s):
        return [pltpu.make_async_copy(leg_hbm.at[s], leg_v.at[s], ls.at[0, s])] + [
            pltpu.make_async_copy(co_hbm.at[k, s], co_v.at[s, :, k * 128 : (k + 1) * 128], ls.at[1 + k, s])
            for k in range(2)
        ]

    pending = [loads(s) for s in range(slots)]
    for copies in pending:
        for copy in copies:
            copy.start()

    barrier = pltpu.get_barrier_semaphore()
    for o in offsets:
        pl.semaphore_signal(barrier, inc=1, device_id=(at(1, o), y), device_id_type=MESH)
    for d in range(1, Y):
        pl.semaphore_signal(barrier, inc=1, device_id=ring(d), device_id_type=MESH)

    def remote(src, dst, send, recv, peer):
        return pltpu.make_async_remote_copy(
            src_ref=src, dst_ref=dst, send_sem=send, recv_sem=recv, device_id=peer, device_id_type=MESH
        )

    degree = lax.broadcasted_iota(jnp.int32, (cycles, degrees), 1)
    sends = {}
    for g in range(GROUPS):
        for t in range(gs):
            s = g * gs + t
            for copy in pending[s]:
                copy.wait()
            order = ord_ref[w * slots + s]
            table = jnp.where(degree >= order, leg_v[s].astype(F32), 0.0).astype(BF16)
            value = dot(table, co_v[s])
            for k in range(2):
                sp[g, pl.ds(k * gs + t, cycles, stride=2 * gs), :] = value[:, k * 128 : (k + 1) * 128]
        if g == 0:
            pl.semaphore_wait(barrier, len(offsets) + Y - 1)
        for r, o in enumerate(offsets):
            to = at(1, o)
            sends[g, r] = remote(
                sp.at[g, pl.ds(pl.multiple_of(to * 2 * gs, 8), 2 * gs), :], rb.at[g, w], s1.at[g, r], r1.at[g, r], (to, y)
            )
            sends[g, r].start()

    orders = row_ref[...]
    weights = jnp.where(orders == 0, 1.0, 2.0).astype(F32)

    def trig(ref, steps, stride, weight):
        turn = orders * (lax.broadcasted_iota(jnp.int32, (steps, total), 0) * stride)
        angle = jnp.bitwise_and(turn, NPIX - 1).astype(F32) * (2.0 * math.pi / NPIX)
        ref[0] = weight * jnp.cos(angle)
        ref[1] = weight * jnp.sin(angle)

    trig(trig_a, HP // SB, SB, weights)
    trig(trig_b, SB, 1, 1.0)
    even = (1 - jnp.bitwise_and(orders, 1)).astype(F32)
    for b in range(total // 128):
        par[b * 128 : (b + 1) * 128, :] = jnp.broadcast_to(even[:, b * 128 : (b + 1) * 128], (128, 128)).T

    def fill(a, carry):
        rows = pl.ds(pl.multiple_of(a * SB, SB), SB)
        ca = trig_a[0, pl.ds(a, 1), :]
        sa = trig_a[1, pl.ds(a, 1), :]
        cb, sb = trig_b[0], trig_b[1]
        for k, value in enumerate((ca * cb - sa * sb, -(sa * cb + ca * sb))):
            hi, lo = split(value)
            th[rows, k * total : (k + 1) * total] = hi
            tl[rows, k * total : (k + 1) * total] = lo
        return carry

    lax.fori_loop(0, HP // SB, fill, 0)

    def prepare(src):
        rows = pl.ds(pl.multiple_of(src * slots, slots), slots)
        evens = par[rows, :]
        for k in range(2):
            value = jnp.concatenate([rb[g, src, k * gs : (k + 1) * gs, :] for g in range(GROUPS)], axis=0)
            own = value * evens
            at_k = pl.ds(pl.multiple_of(k * total + src * slots, slots), slots)
            for p, part in enumerate((own, value - own)):
                hi, lo = split(part)
                rhs[at_k, p * 128 : (p + 1) * 128] = hi
                rhs[at_k, 256 + p * 128 : 256 + (p + 1) * 128] = lo

    for g in range(GROUPS):
        rb[g, w] = sp[g, pl.ds(pl.multiple_of(w * 2 * gs, 8), 2 * gs), :]
    prepare(w)
    for r, o in enumerate(offsets):
        for g in range(GROUPS):
            sends[g, r].wait_recv()
        prepare(at(-1, o))

    width = NPIX // Y
    sub = width // SUBS
    outs = {}
    for d in (2, 1):
        first = lax.rem(y + d, Y)
        sign = jnp.where(first < Y // 2, 1.0, -1.0).astype(F32)
        start = lax.rem(first, Y // 2) * width
        for b in range(SUBS):
            rows = pl.ds(pl.multiple_of(start + b * sub, sub), sub)
            top = dot(th[rows, :], rhs[...])
            low = dot(tl[rows, :], rhs[:, 0:256])
            e = top[:, 0:128] + top[:, 256:384] + low[:, 0:128]
            o = sign * (top[:, 128:256] + top[:, 384:512] + low[:, 128:256])
            for q, value in ((d, e + o), ((d + 2) % Y, e - o)):
                mine = slice(b * sub, (b + 1) * sub)
                if q == 0:
                    out_ref[y, mine, :] = value
                else:
                    stage[q - 1, mine, :] = value
                    outs[q, b] = remote(
                        stage.at[q - 1, mine, :], out_ref.at[y, mine, :], s2.at[q, b], r2.at[q, b], ring(q)
                    )
                    outs[q, b].start()
    for copy in outs.values():
        copy.wait_recv()
    for copy in outs.values():
        copy.wait_send()
    for copy in sends.values():
        copy.wait_send()


def front_stage(order_table, legendre, coeffs):
    slots, cycles, degrees = legendre.shape
    total = WIDE * slots
    gs = slots // GROUPS
    width = NPIX // Y
    dma = pltpu.SemaphoreType.DMA
    hbm = pl.BlockSpec(memory_space=pl.ANY)
    return pl.pallas_call(
        front_kernel,
        name="front_stage",
        out_shape=jax.ShapeDtypeStruct((Y, width, 128), F32),
        in_specs=[SM, VM, hbm, hbm],
        out_specs=VM,
        scratch_shapes=[
            pltpu.VMEM((slots, cycles, degrees), BF16),
            pltpu.VMEM((slots, degrees, 256), BF16),
            pltpu.VMEM((GROUPS, cycles * 2 * gs, 128), F32),
            pltpu.VMEM((GROUPS, WIDE, 2 * gs, 128), F32),
            pltpu.VMEM((HP, 2 * total), BF16),
            pltpu.VMEM((HP, 2 * total), BF16),
            pltpu.VMEM((2, HP // SB, total), F32),
            pltpu.VMEM((2, SB, total), F32),
            pltpu.VMEM((total, 128), F32),
            pltpu.VMEM((2 * total, 512), BF16),
            pltpu.VMEM((Y - 1, width, 128), F32),
            dma((3, slots)),
            dma((GROUPS, WIDE)),
            dma((GROUPS, WIDE)),
            dma((Y, SUBS)),
            dma((Y, SUBS)),
        ],
        compiler_params=pltpu.CompilerParams(collective_id=1, has_side_effects=True),
    )(order_table, order_table[None, :], legendre, coeffs)


def per_device(coeffs, legendre, order_table, thresholds):
    parts = front_stage(order_table, legendre, coeffs)
    thr = thresholds[None, :]
    scales = jnp.asarray(SCALES + [0.0] * (16 - len(SCALES)), F32)
    sky, res, cov = first_stage(parts, thr)
    sparse, res, cov = middle_stage(scales, cov, res, sky, thr)
    low, sparse = last_stage(scales, cov, res, sparse)
    return low[None], sparse[None]


def solution(mesh):
    placed = (P(None, "wide", None, "narrow"), P("wide", None, None), P(), P())
    return jax.shard_map(
        per_device,
        mesh=mesh,
        in_specs=placed,
        out_specs=(P("wide", "narrow", None), P("wide", "narrow", None)),
        check_vma=False,
    )
```

```python
import functools
import math

import jax
import jax.numpy as jnp
from jax import lax
from jax.experimental import pallas as pl
from jax.experimental.pallas import tpu as pltpu
from jax.sharding import PartitionSpec as P

MESH = pl.DeviceIdType.MESH
F32 = jnp.float32
BF16 = jnp.bfloat16

NPIX = 2048
NCH = 512
NB = 4
PAIRS = [(i, j) for i in range(NB) for j in range(i, NB)]
ROWS = 128 * len(PAIRS)
HALF = ROWS // 2
X, Y, Z = 4, 4, 8
CHUNK = HALF // (X * Y)
LIMIT = 64 * 1024 * 1024 - 65536 - 8192

KAPPA = NCH + 1.0
OMEGA = 2.0 / (KAPPA + 1.0)


def newton_scales():
    delta = (KAPPA - 1.0) / (KAPPA + 1.0)
    scales = []
    while delta > 1e-2:
        scales.append(2.0 / (2.0 - delta * delta))
        delta = delta * delta / (2.0 - delta * delta)
    return scales


SCALES = newton_scales()


def split(x):
    hi = x.astype(BF16)
    return hi, (x - hi.astype(F32)).astype(BF16)


def dot(a, b):
    return jnp.dot(a, b, preferred_element_type=F32)


def put_left(ref, x):
    n = x.shape[1]
    hi, lo = split(x)
    ref[:, 0:n] = hi
    ref[:, n : 2 * n] = lo
    ref[:, 2 * n : 3 * n] = hi


def put_right(ref, x):
    n = x.shape[0]
    hi, lo = split(x)
    ref[0:n, :] = hi
    ref[n : 2 * n, :] = hi
    ref[2 * n : 3 * n, :] = lo


def reduce_peers():
    w = lax.axis_index("wide")
    y = lax.axis_index("narrow")
    core = lax.rem(w, 2)
    x = lax.rem(w // 2, X)
    z = w // (2 * X)
    other = 1 - core
    partner = (w + 1 - 2 * core, y)

    def plane(k):
        dx, dy = k // Y, k % Y
        px, py = lax.rem(x + dx, X), lax.rem(y + dy, Y)
        return (z * 2 * X + px * 2 + core, py), px * Y + py

    def deep(d):
        return (lax.rem(z + d, Z) * 2 * X + x * 2 + core, y)

    return x, y, core, other, partner, plane, deep


def greet():
    _, _, _, _, partner, plane, deep = reduce_peers()
    barrier = pltpu.get_barrier_semaphore()
    for peer in [partner] + [plane(k)[0] for k in range(1, X * Y)] + [deep(d) for d in range(1, Z)]:
        pl.semaphore_signal(barrier, inc=1, device_id=peer, device_id_type=MESH)


def reduce_all(p_ref, out_ref, b1, acc1, b2, acc2, b3, acc3, s1, r1, s2, r2, s3, r3, s4, r4, s5, r5):
    x, y, core, other, partner, plane, deep = reduce_peers()
    pl.semaphore_wait(pltpu.get_barrier_semaphore(), X * Y + Z - 1)

    order = sorted(range(X * Y), key=lambda k: -(min(k // Y, X - k // Y) + min(k % Y, Y - k % Y)))

    def rows(side, g):
        return pl.ds(pl.multiple_of(side * HALF + g * CHUNK, 8), CHUNK)

    def remote(src, dst, send, recv, peer):
        return pltpu.make_async_remote_copy(
            src_ref=src, dst_ref=dst, send_sem=send, recv_sem=recv, device_id=peer, device_id_type=MESH
        )

    first, second = {}, {}
    for k in order:
        first[k] = remote(p_ref.at[rows(other, plane(k)[1])], b1.at[k], s1.at[k], r1.at[k], partner)
        first[k].start()
    for k in order:
        peer, g = plane(k)
        first[k].wait_recv()
        acc1[k] = p_ref[rows(core, g)] + b1[k]
        if k:
            second[k] = remote(acc1.at[k], b2.at[k], s2.at[k], r2.at[k], peer)
            second[k].start()
    total = acc1[0]
    for k in order:
        if k:
            second[k].wait_recv()
            total = total + b2[k]
    acc2[...] = total
    third = {}
    for d in (4, 3, 5, 2, 6, 1, 7):
        third[d] = remote(acc2, b3.at[d], s3.at[d], r3.at[d], deep(d))
        third[d].start()
    total = acc2[...]
    for d in (1, 7, 2, 6, 3, 5, 4):
        third[d].wait_recv()
        total = total + b3[d]
    acc3[...] = total
    mine = rows(core, x * Y + y)
    fourth, fifth = {}, {}
    for k in order:
        if k:
            fourth[k] = remote(acc3, out_ref.at[mine], s4.at[k], r4.at[k], plane(k)[0])
            fourth[k].start()
    fifth[0] = remote(acc3, out_ref.at[mine], s5.at[0], r5.at[0], partner)
    fifth[0].start()
    out_ref[mine] = total
    for k in reversed(order):
        if k:
            px, py = lax.rem(x + X - k // Y, X), lax.rem(y + Y - k % Y, Y)
            got = rows(core, px * Y + py)
            fourth[k].wait_recv()
            fifth[k] = remote(out_ref.at[got], out_ref.at[got], s5.at[k], r5.at[k], partner)
            fifth[k].start()
    for k in order:
        fifth[k].wait_recv()
    for k in order:
        first[k].wait_send()
        fifth[k].wait_send()
        if k:
            second[k].wait_send()
            fourth[k].wait_send()
    for d in range(1, Z):
        third[d].wait_send()


def reduce_scratch():
    n = X * Y
    dma = pltpu.SemaphoreType.DMA
    return (
        [
            pltpu.VMEM((ROWS, 128), F32),
            pltpu.VMEM((n, CHUNK, 128), F32),
            pltpu.VMEM((n, CHUNK, 128), F32),
            pltpu.VMEM((n, CHUNK, 128), F32),
            pltpu.VMEM((CHUNK, 128), F32),
            pltpu.VMEM((Z, CHUNK, 128), F32),
            pltpu.VMEM((CHUNK, 128), F32),
        ]
        + [dma((n,))] * 4
        + [dma((Z,))] * 2
        + [dma((n,))] * 4
    )


def put_cov(res, cov_ref, left, right):
    put_right(left, res)
    n = res.shape[0]
    right[0:n, :] = left[0:n, :]
    right[n : 2 * n, :] = left[2 * n : 3 * n, :]
    right[2 * n : 3 * n, :] = left[0:n, :]
    at = 0
    for i in range(NB):
        width = (NB - i) * 128
        rows = lax.dot_general(
            left[:, i * 128 : (i + 1) * 128],
            right[:, i * 128 :],
            (((0,), (0,)), ((), ())),
            preferred_element_type=F32,
        )
        for b in range(NB - i):
            cov_ref[at : at + 128, :] = rows[:, b * 128 : (b + 1) * 128]
            at += 128


def moves(pairs, sems):
    copies = [pltpu.make_async_copy(src, dst, sems.at[i]) for i, (src, dst) in enumerate(pairs)]
    for copy in copies:
        copy.start()
    return copies


def first_kernel(parts_ref, thr_ref, sky_out, res_out, cov_ref, left, right, sky_ref, res_ref, sems, part_ref, *reduce_refs):
    greet()
    thr = thr_ref[...]
    sky = jnp.concatenate([parts_ref[i] for i in range(NB)], axis=1)
    sky_ref[...] = sky
    res = sky - (sky - jnp.minimum(jnp.maximum(sky, -thr), thr))
    res_ref[...] = res
    put_cov(res, part_ref, left, right)
    outs = moves(((sky_ref, sky_out), (res_ref, res_out)), sems)
    reduce_all(part_ref, cov_ref, *reduce_refs)
    for copy in outs:
        copy.wait()


def put_inverse(cov_ref, scales_ref, a_ref, x_ref, a3, xl, xr, wl):
    eye = (lax.broadcasted_iota(jnp.int32, (128, 128), 0) == lax.broadcasted_iota(jnp.int32, (128, 128), 1)).astype(F32)
    diag = jnp.zeros((128, 128), F32)
    for idx, (i, j) in enumerate(PAIRS):
        if i == j:
            diag = diag + cov_ref[idx * 128 : (idx + 1) * 128, :] * eye
    total = jnp.sum(jnp.sum(diag, axis=0, keepdims=True), axis=1, keepdims=True)
    inv_t = float(NCH) / total
    for idx, (i, j) in enumerate(PAIRS):
        block = cov_ref[idx * 128 : (idx + 1) * 128, :] * inv_t
        if i == j:
            block = block + eye
            a_ref[i * 128 : (i + 1) * 128, i * 128 : (i + 1) * 128] = block
        else:
            a_ref[i * 128 : (i + 1) * 128, j * 128 : (j + 1) * 128] = block
            a_ref[j * 128 : (j + 1) * 128, i * 128 : (i + 1) * 128] = block.T
    a = a_ref[...]
    put_right(a3, a)
    full_eye = (
        lax.broadcasted_iota(jnp.int32, (NCH, NCH), 0) == lax.broadcasted_iota(jnp.int32, (NCH, NCH), 1)
    ).astype(F32)
    x = (SCALES[0] * OMEGA) * (2.0 * full_eye - OMEGA * a)
    x_ref[...] = x
    put_left(xl, x)
    put_right(xr, x)

    def step(k, carry):
        wa = dot(xl[...], a3[...])
        put_left(wl, wa)
        x = scales_ref[k] * (2.0 * x_ref[...] - dot(wl[...], xr[...]))
        x_ref[...] = x
        put_left(xl, x)
        put_right(xr, x)
        return carry

    lax.fori_loop(1, len(SCALES), step, 0)
    x = x_ref[...]
    rest = full_eye - jnp.dot(x, a_ref[...], preferred_element_type=F32, precision=lax.Precision.HIGHEST)
    put_left(wl, rest)
    put_right(a3, x + dot(wl[:, 0:NCH], xr[0:NCH, :]))
    put_right(xr, x + dot(wl[...], a3[...]))


def low_of(res_ref, xl, xr):
    res = res_ref[...]
    put_left(xl, res)
    return res - dot(xl[...], xr[...])


def middle_kernel(
    scales_ref, cov_ref, res_in, sky_in, thr_ref, sparse_out, res2_out, cov2_ref,
    a_ref, x_ref, a3, xl, xr, wl, res_ref, sky_ref, sparse_ref, res2_ref, in_sems, out_sems, part_ref, *reduce_refs,
):
    ins = moves(((res_in, res_ref), (sky_in, sky_ref)), in_sems)
    greet()
    put_inverse(cov_ref, scales_ref, a_ref, x_ref, a3, xl, xr, wl)
    for copy in ins:
        copy.wait()
    thr = thr_ref[...]
    sky = sky_ref[...]
    v = sky - low_of(res_ref, xl, xr)
    sparse = v - jnp.minimum(jnp.maximum(v, -thr), thr)
    sparse_ref[...] = sparse
    res = sky - sparse
    res2_ref[...] = res
    put_cov(res, part_ref, a3, xr)
    outs = moves(((sparse_ref, sparse_out), (res2_ref, res2_out)), out_sems)
    reduce_all(part_ref, cov2_ref, *reduce_refs)
    for copy in outs:
        copy.wait()


def last_kernel(
    scales_ref, cov_ref, res_in, sparse_in, low_ref, sparse_out,
    a_ref, x_ref, a3, xl, xr, wl, res_ref, sparse_ref, in_sems, out_sems,
):
    ins = moves(((res_in, res_ref), (sparse_in, sparse_ref)), in_sems)
    put_inverse(cov_ref, scales_ref, a_ref, x_ref, a3, xl, xr, wl)
    for copy in ins:
        copy.wait()
    outs = moves(((sparse_ref, sparse_out),), out_sems)
    low_ref[...] = low_of(res_ref, xl, xr)
    outs[0].wait()


VM = pl.BlockSpec(memory_space=pltpu.VMEM)
SM = pl.BlockSpec(memory_space=pltpu.SMEM)
HBM = pl.BlockSpec(memory_space=pl.ANY)


def inverse_scratch():
    return [
        pltpu.VMEM((NCH, NCH), F32),
        pltpu.VMEM((NCH, NCH), F32),
        pltpu.VMEM((3 * NCH, NCH), BF16),
        pltpu.VMEM((NCH, 3 * NCH), BF16),
        pltpu.VMEM((3 * NCH, NCH), BF16),
        pltpu.VMEM((NCH, 3 * NCH), BF16),
    ]


def first_stage(parts, thr):
    pix = parts.shape[1]
    return pl.pallas_call(
        first_kernel,
        name="first_stage",
        out_shape=(
            jax.ShapeDtypeStruct((pix, NCH), F32),
            jax.ShapeDtypeStruct((pix, NCH), F32),
            jax.ShapeDtypeStruct((ROWS, 128), F32),
        ),
        in_specs=[VM, VM],
        out_specs=(HBM, HBM, VM),
        scratch_shapes=[pltpu.VMEM((3 * pix, NCH), BF16)] * 2
        + [pltpu.VMEM((pix, NCH), F32)] * 2
        + [pltpu.SemaphoreType.DMA((2,))]
        + reduce_scratch(),
        compiler_params=pltpu.CompilerParams(collective_id=2, has_side_effects=True),
    )(parts, thr)


def middle_stage(scales, cov, res, sky, thr):
    pix = sky.shape[0]
    return pl.pallas_call(
        middle_kernel,
        name="middle_stage",
        out_shape=(
            jax.ShapeDtypeStruct((pix, NCH), F32),
            jax.ShapeDtypeStruct((pix, NCH), F32),
            jax.ShapeDtypeStruct((ROWS, 128), F32),
        ),
        in_specs=[SM, VM, HBM, HBM, VM],
        out_specs=(HBM, HBM, VM),
        scratch_shapes=inverse_scratch()
        + [pltpu.VMEM((pix, NCH), F32)] * 4
        + [pltpu.SemaphoreType.DMA((2,))] * 2
        + reduce_scratch(),
        compiler_params=pltpu.CompilerParams(collective_id=3, has_side_effects=True),
    )(scales, cov, res, sky, thr)


def last_stage(scales, cov, res, sparse):
    return pl.pallas_call(
        last_kernel,
        name="last_stage",
        out_shape=(jax.ShapeDtypeStruct(res.shape, F32), jax.ShapeDtypeStruct(res.shape, F32)),
        in_specs=[SM, VM, HBM, HBM],
        out_specs=(VM, HBM),
        scratch_shapes=inverse_scratch()
        + [pltpu.VMEM(res.shape, F32)] * 2
        + [pltpu.SemaphoreType.DMA((2,)), pltpu.SemaphoreType.DMA((1,))],
    )(scales, cov, res, sparse)


SB = 64
HP = NPIX // 2
WIDE = 2 * X * Z
GROUPS = 2
SUBS = 2


def front_kernel(
    ord_ref, row_ref, leg_hbm, co_hbm, out_ref,
    leg_v, co_v, sp, rb, th, tl, trig_a, trig_b, par, rhs, stage,
    ls, s1, r1, s2, r2,
):
    slots, cycles, degrees = leg_v.shape
    total = WIDE * slots
    gs = slots // GROUPS
    w = lax.axis_index("wide")
    y = lax.axis_index("narrow")
    core = lax.rem(w, 2)
    x = lax.rem(w // 2, X)
    z = w // (2 * X)

    offsets = [(dz, dx, dc) for dz in range(Z) for dx in range(X) for dc in range(2)][1:]
    offsets.sort(key=lambda o: (-min(o[0], Z - o[0]) - min(o[1], X - o[1]), o[1], o[2], o[0]))

    def at(sign, o):
        dz, dx, dc = o
        pz = lax.rem(z + (dz if sign > 0 else Z - dz), Z)
        px = lax.rem(x + (dx if sign > 0 else X - dx), X)
        return pz * 2 * X + px * 2 + (lax.rem(core + dc, 2))

    def ring(d):
        return (w, lax.rem(y + d, Y))

    def loads(s):
        return [pltpu.make_async_copy(leg_hbm.at[s], leg_v.at[s], ls.at[0, s])] + [
            pltpu.make_async_copy(co_hbm.at[k, s], co_v.at[s, :, k * 128 : (k + 1) * 128], ls.at[1 + k, s])
            for k in range(2)
        ]

    pending = [loads(s) for s in range(slots)]
    for copies in pending:
        for copy in copies:
            copy.start()

    barrier = pltpu.get_barrier_semaphore()
    for o in offsets:
        pl.semaphore_signal(barrier, inc=1, device_id=(at(1, o), y), device_id_type=MESH)
    for d in range(1, Y):
        pl.semaphore_signal(barrier, inc=1, device_id=ring(d), device_id_type=MESH)

    def remote(src, dst, send, recv, peer):
        return pltpu.make_async_remote_copy(
            src_ref=src, dst_ref=dst, send_sem=send, recv_sem=recv, device_id=peer, device_id_type=MESH
        )

    degree = lax.broadcasted_iota(jnp.int32, (cycles, degrees), 1)
    sends = {}
    for g in range(GROUPS):
        for t in range(gs):
            s = g * gs + t
            for copy in pending[s]:
                copy.wait()
            order = ord_ref[w * slots + s]
            table = jnp.where(degree >= order, leg_v[s].astype(F32), 0.0).astype(BF16)
            value = dot(table, co_v[s])
            for k in range(2):
                sp[g, pl.ds(k * gs + t, cycles, stride=2 * gs), :] = value[:, k * 128 : (k + 1) * 128]
        if g == 0:
            pl.semaphore_wait(barrier, len(offsets) + Y - 1)
        for r, o in enumerate(offsets):
            to = at(1, o)
            sends[g, r] = remote(
                sp.at[g, pl.ds(pl.multiple_of(to * 2 * gs, 8), 2 * gs), :], rb.at[g, w], s1.at[g, r], r1.at[g, r], (to, y)
            )
            sends[g, r].start()

    orders = row_ref[...]
    weights = jnp.where(orders == 0, 1.0, 2.0).astype(F32)

    def trig(ref, steps, stride, weight):
        turn = orders * (lax.broadcasted_iota(jnp.int32, (steps, total), 0) * stride)
        angle = jnp.bitwise_and(turn, NPIX - 1).astype(F32) * (2.0 * math.pi / NPIX)
        ref[0] = weight * jnp.cos(angle)
        ref[1] = weight * jnp.sin(angle)

    trig(trig_a, HP // SB, SB, weights)
    trig(trig_b, SB, 1, 1.0)
    even = (1 - jnp.bitwise_and(orders, 1)).astype(F32)
    for b in range(total // 128):
        par[b * 128 : (b + 1) * 128, :] = jnp.broadcast_to(even[:, b * 128 : (b + 1) * 128], (128, 128)).T

    def fill(a, carry):
        rows = pl.ds(pl.multiple_of(a * SB, SB), SB)
        ca = trig_a[0, pl.ds(a, 1), :]
        sa = trig_a[1, pl.ds(a, 1), :]
        cb, sb = trig_b[0], trig_b[1]
        for k, value in enumerate((ca * cb - sa * sb, -(sa * cb + ca * sb))):
            hi, lo = split(value)
            th[rows, k * total : (k + 1) * total] = hi
            tl[rows, k * total : (k + 1) * total] = lo
        return carry

    lax.fori_loop(0, HP // SB, fill, 0)

    def prepare(src):
        rows = pl.ds(pl.multiple_of(src * slots, slots), slots)
        evens = par[rows, :]
        for k in range(2):
            value = jnp.concatenate([rb[g, src, k * gs : (k + 1) * gs, :] for g in range(GROUPS)], axis=0)
            own = value * evens
            at_k = pl.ds(pl.multiple_of(k * total + src * slots, slots), slots)
            for p, part in enumerate((own, value - own)):
                hi, lo = split(part)
                rhs[at_k, p * 128 : (p + 1) * 128] = hi
                rhs[at_k, 256 + p * 128 : 256 + (p + 1) * 128] = lo

    for g in range(GROUPS):
        rb[g, w] = sp[g, pl.ds(pl.multiple_of(w * 2 * gs, 8), 2 * gs), :]
    prepare(w)
    for r, o in enumerate(offsets):
        for g in range(GROUPS):
            sends[g, r].wait_recv()
        prepare(at(-1, o))

    width = NPIX // Y
    sub = width // SUBS
    outs = {}
    for d in (2, 1):
        first = lax.rem(y + d, Y)
        sign = jnp.where(first < Y // 2, 1.0, -1.0).astype(F32)
        start = lax.rem(first, Y // 2) * width
        for b in range(SUBS):
            rows = pl.ds(pl.multiple_of(start + b * sub, sub), sub)
            top = dot(th[rows, :], rhs[...])
            low = dot(tl[rows, :], rhs[:, 0:256])
            e = top[:, 0:128] + top[:, 256:384] + low[:, 0:128]
            o = sign * (top[:, 128:256] + top[:, 384:512] + low[:, 128:256])
            for q, value in ((d, e + o), ((d + 2) % Y, e - o)):
                mine = slice(b * sub, (b + 1) * sub)
                if q == 0:
                    out_ref[y, mine, :] = value
                else:
                    stage[q - 1, mine, :] = value
                    outs[q, b] = remote(
                        stage.at[q - 1, mine, :], out_ref.at[y, mine, :], s2.at[q, b], r2.at[q, b], ring(q)
                    )
                    outs[q, b].start()
    for copy in outs.values():
        copy.wait_recv()
    for copy in outs.values():
        copy.wait_send()
    for copy in sends.values():
        copy.wait_send()


def front_stage(order_table, legendre, coeffs):
    slots, cycles, degrees = legendre.shape
    total = WIDE * slots
    gs = slots // GROUPS
    width = NPIX // Y
    dma = pltpu.SemaphoreType.DMA
    hbm = pl.BlockSpec(memory_space=pl.ANY)
    return pl.pallas_call(
        front_kernel,
        name="front_stage",
        out_shape=jax.ShapeDtypeStruct((Y, width, 128), F32),
        in_specs=[SM, VM, hbm, hbm],
        out_specs=VM,
        scratch_shapes=[
            pltpu.VMEM((slots, cycles, degrees), BF16),
            pltpu.VMEM((slots, degrees, 256), BF16),
            pltpu.VMEM((GROUPS, cycles * 2 * gs, 128), F32),
            pltpu.VMEM((GROUPS, WIDE, 2 * gs, 128), F32),
            pltpu.VMEM((HP, 2 * total), BF16),
            pltpu.VMEM((HP, 2 * total), BF16),
            pltpu.VMEM((2, HP // SB, total), F32),
            pltpu.VMEM((2, SB, total), F32),
            pltpu.VMEM((total, 128), F32),
            pltpu.VMEM((2 * total, 512), BF16),
            pltpu.VMEM((Y - 1, width, 128), F32),
            dma((3, slots)),
            dma((GROUPS, WIDE)),
            dma((GROUPS, WIDE)),
            dma((Y, SUBS)),
            dma((Y, SUBS)),
        ],
        compiler_params=pltpu.CompilerParams(collective_id=1, has_side_effects=True),
    )(order_table, order_table[None, :], legendre, coeffs)


def per_device(coeffs, legendre, order_table, thresholds):
    parts = front_stage(order_table, legendre, coeffs)
    thr = thresholds[None, :]
    scales = jnp.asarray(SCALES + [0.0] * (16 - len(SCALES)), F32)
    sky, res, cov = first_stage(parts, thr)
    sparse, res, cov = middle_stage(scales, cov, res, sky, thr)
    low, sparse = last_stage(scales, cov, res, sparse)
    return low[None], sparse[None]


def solution(mesh):
    placed = (P(None, "wide", None, "narrow"), P("wide", None, None), P(), P())
    return jax.shard_map(
        per_device,
        mesh=mesh,
        in_specs=placed,
        out_specs=(P("wide", "narrow", None), P("wide", "narrow", None)),
        check_vma=False,
    )
```

```python
import functools
import math

import jax
import jax.numpy as jnp
from jax import lax
from jax.experimental import pallas as pl
from jax.experimental.pallas import tpu as pltpu
from jax.sharding import PartitionSpec as P

MESH = pl.DeviceIdType.MESH
F32 = jnp.float32
BF16 = jnp.bfloat16

NPIX = 2048
NCH = 512
NB = 4
PAIRS = [(i, j) for i in range(NB) for j in range(i, NB)]
ROWS = 128 * len(PAIRS)
HALF = ROWS // 2
X, Y, Z = 4, 4, 8
CHUNK = HALF // (X * Y)
LIMIT = 64 * 1024 * 1024 - 65536 - 8192

KAPPA = NCH + 1.0
OMEGA = 2.0 / (KAPPA + 1.0)


def newton_scales():
    delta = (KAPPA - 1.0) / (KAPPA + 1.0)
    scales = []
    while delta > 1e-2:
        scales.append(2.0 / (2.0 - delta * delta))
        delta = delta * delta / (2.0 - delta * delta)
    return scales


SCALES = newton_scales()


def split(x):
    hi = x.astype(BF16)
    return hi, (x - hi.astype(F32)).astype(BF16)


def dot(a, b):
    return jnp.dot(a, b, preferred_element_type=F32)


def put_left(ref, x):
    n = x.shape[1]
    hi, lo = split(x)
    ref[:, 0:n] = hi
    ref[:, n : 2 * n] = lo
    ref[:, 2 * n : 3 * n] = hi


def put_right(ref, x):
    n = x.shape[0]
    hi, lo = split(x)
    ref[0:n, :] = hi
    ref[n : 2 * n, :] = hi
    ref[2 * n : 3 * n, :] = lo


def reduce_peers():
    w = lax.axis_index("wide")
    y = lax.axis_index("narrow")
    core = lax.rem(w, 2)
    x = lax.rem(w // 2, X)
    z = w // (2 * X)
    other = 1 - core
    partner = (w + 1 - 2 * core, y)

    def plane(k):
        dx, dy = k // Y, k % Y
        px, py = lax.rem(x + dx, X), lax.rem(y + dy, Y)
        return (z * 2 * X + px * 2 + core, py), px * Y + py

    def deep(d):
        return (lax.rem(z + d, Z) * 2 * X + x * 2 + core, y)

    return x, y, core, other, partner, plane, deep


GREETED = X * Y + Z - 1


def greet():
    _, _, _, _, partner, plane, deep = reduce_peers()
    barrier = pltpu.get_barrier_semaphore()
    for peer in [partner] + [plane(k)[0] for k in range(1, X * Y)] + [deep(d) for d in range(1, Z)]:
        pl.semaphore_signal(barrier, inc=1, device_id=peer, device_id_type=MESH)


def reduce_all(p_ref, out_ref, b1, acc1, b2, acc2, b3, acc3, s1, r1, s2, r2, s3, r3, s4, r4, s5, r5):
    x, y, core, other, partner, plane, deep = reduce_peers()

    order = sorted(range(X * Y), key=lambda k: -(min(k // Y, X - k // Y) + min(k % Y, Y - k % Y)))

    def rows(side, g):
        return pl.ds(pl.multiple_of(side * HALF + g * CHUNK, 8), CHUNK)

    def remote(src, dst, send, recv, peer):
        return pltpu.make_async_remote_copy(
            src_ref=src, dst_ref=dst, send_sem=send, recv_sem=recv, device_id=peer, device_id_type=MESH
        )

    first, second = {}, {}
    for k in order:
        first[k] = remote(p_ref.at[rows(other, plane(k)[1])], b1.at[k], s1.at[k], r1.at[k], partner)
        first[k].start()
    for k in order:
        peer, g = plane(k)
        first[k].wait_recv()
        acc1[k] = p_ref[rows(core, g)] + b1[k]
        if k:
            second[k] = remote(acc1.at[k], b2.at[k], s2.at[k], r2.at[k], peer)
            second[k].start()
    total = acc1[0]
    for k in order:
        if k:
            second[k].wait_recv()
            total = total + b2[k]
    acc2[...] = total
    third = {}
    for d in (4, 3, 5, 2, 6, 1, 7):
        third[d] = remote(acc2, b3.at[d], s3.at[d], r3.at[d], deep(d))
        third[d].start()
    total = acc2[...]
    for d in (1, 7, 2, 6, 3, 5, 4):
        third[d].wait_recv()
        total = total + b3[d]
    acc3[...] = total
    mine = rows(core, x * Y + y)
    fourth, fifth = {}, {}
    for k in order:
        if k:
            fourth[k] = remote(acc3, out_ref.at[mine], s4.at[k], r4.at[k], plane(k)[0])
            fourth[k].start()
    fifth[0] = remote(acc3, out_ref.at[mine], s5.at[0], r5.at[0], partner)
    fifth[0].start()
    out_ref[mine] = total
    for k in reversed(order):
        if k:
            px, py = lax.rem(x + X - k // Y, X), lax.rem(y + Y - k % Y, Y)
            got = rows(core, px * Y + py)
            fourth[k].wait_recv()
            fifth[k] = remote(out_ref.at[got], out_ref.at[got], s5.at[k], r5.at[k], partner)
            fifth[k].start()
    for k in order:
        fifth[k].wait_recv()
    for k in order:
        first[k].wait_send()
        fifth[k].wait_send()
        if k:
            second[k].wait_send()
            fourth[k].wait_send()
    for d in range(1, Z):
        third[d].wait_send()


def reduce_scratch():
    n = X * Y
    dma = pltpu.SemaphoreType.DMA
    return (
        [
            pltpu.VMEM((ROWS, 128), F32),
            pltpu.VMEM((n, CHUNK, 128), F32),
            pltpu.VMEM((n, CHUNK, 128), F32),
            pltpu.VMEM((n, CHUNK, 128), F32),
            pltpu.VMEM((CHUNK, 128), F32),
            pltpu.VMEM((Z, CHUNK, 128), F32),
            pltpu.VMEM((CHUNK, 128), F32),
        ]
        + [dma((n,))] * 4
        + [dma((Z,))] * 2
        + [dma((n,))] * 4
    )


def put_cov(res, cov_ref, left, right):
    put_right(left, res)
    n = res.shape[0]
    right[0:n, :] = left[0:n, :]
    right[n : 2 * n, :] = left[2 * n : 3 * n, :]
    right[2 * n : 3 * n, :] = left[0:n, :]
    at = 0
    for i in range(NB):
        width = (NB - i) * 128
        rows = lax.dot_general(
            left[:, i * 128 : (i + 1) * 128],
            right[:, i * 128 :],
            (((0,), (0,)), ((), ())),
            preferred_element_type=F32,
        )
        for b in range(NB - i):
            cov_ref[at : at + 128, :] = rows[:, b * 128 : (b + 1) * 128]
            at += 128


def moves(pairs, sems):
    copies = [pltpu.make_async_copy(src, dst, sems.at[i]) for i, (src, dst) in enumerate(pairs)]
    for copy in copies:
        copy.start()
    return copies


def first_body(parts_ref, thr_ref, sky_out, res_out, cov_ref, left, right, sky_ref, res_ref, sems, part_ref, *reduce_refs):
    thr = thr_ref[...]
    sky = jnp.concatenate([parts_ref[i] for i in range(NB)], axis=1)
    sky_ref[...] = sky
    res = sky - (sky - jnp.minimum(jnp.maximum(sky, -thr), thr))
    res_ref[...] = res
    put_cov(res, part_ref, left, right)
    outs = moves(((sky_ref, sky_out), (res_ref, res_out)), sems)
    reduce_all(part_ref, cov_ref, *reduce_refs)
    for copy in outs:
        copy.wait()


def put_inverse(cov_ref, scales_ref, a_ref, x_ref, a3, xl, xr, wl):
    eye = (lax.broadcasted_iota(jnp.int32, (128, 128), 0) == lax.broadcasted_iota(jnp.int32, (128, 128), 1)).astype(F32)
    diag = jnp.zeros((128, 128), F32)
    for idx, (i, j) in enumerate(PAIRS):
        if i == j:
            diag = diag + cov_ref[idx * 128 : (idx + 1) * 128, :] * eye
    total = jnp.sum(jnp.sum(diag, axis=0, keepdims=True), axis=1, keepdims=True)
    inv_t = float(NCH) / total
    for idx, (i, j) in enumerate(PAIRS):
        block = cov_ref[idx * 128 : (idx + 1) * 128, :] * inv_t
        if i == j:
            block = block + eye
            a_ref[i * 128 : (i + 1) * 128, i * 128 : (i + 1) * 128] = block
        else:
            a_ref[i * 128 : (i + 1) * 128, j * 128 : (j + 1) * 128] = block
            a_ref[j * 128 : (j + 1) * 128, i * 128 : (i + 1) * 128] = block.T
    a = a_ref[...]
    put_right(a3, a)
    full_eye = (
        lax.broadcasted_iota(jnp.int32, (NCH, NCH), 0) == lax.broadcasted_iota(jnp.int32, (NCH, NCH), 1)
    ).astype(F32)
    x = (SCALES[0] * OMEGA) * (2.0 * full_eye - OMEGA * a)
    x_ref[...] = x
    put_left(xl, x)
    put_right(xr, x)

    def step(k, carry):
        wa = dot(xl[...], a3[...])
        put_left(wl, wa)
        x = scales_ref[k] * (2.0 * x_ref[...] - dot(wl[...], xr[...]))
        x_ref[...] = x
        put_left(xl, x)
        put_right(xr, x)
        return carry

    lax.fori_loop(1, len(SCALES), step, 0)
    x = x_ref[...]
    rest = full_eye - jnp.dot(x, a_ref[...], preferred_element_type=F32, precision=lax.Precision.HIGHEST)
    put_left(wl, rest)
    put_right(a3, x + dot(wl[:, 0:NCH], xr[0:NCH, :]))
    put_right(xr, x + dot(wl[...], a3[...]))


def low_of(res_ref, xl, xr):
    res = res_ref[...]
    put_left(xl, res)
    return res - dot(xl[...], xr[...])


def middle_kernel(
    scales_ref, cov_ref, res_in, sky_in, thr_ref, sparse_out, res2_out, cov2_ref,
    a_ref, x_ref, a3, xl, xr, wl, res_ref, sky_ref, sparse_ref, res2_ref, in_sems, out_sems, part_ref, *reduce_refs,
):
    ins = moves(((res_in, res_ref), (sky_in, sky_ref)), in_sems)
    greet()
    put_inverse(cov_ref, scales_ref, a_ref, x_ref, a3, xl, xr, wl)
    for copy in ins:
        copy.wait()
    thr = thr_ref[...]
    sky = sky_ref[...]
    v = sky - low_of(res_ref, xl, xr)
    sparse = v - jnp.minimum(jnp.maximum(v, -thr), thr)
    sparse_ref[...] = sparse
    res = sky - sparse
    res2_ref[...] = res
    put_cov(res, part_ref, a3, xr)
    outs = moves(((sparse_ref, sparse_out), (res2_ref, res2_out)), out_sems)
    pl.semaphore_wait(pltpu.get_barrier_semaphore(), GREETED)
    reduce_all(part_ref, cov2_ref, *reduce_refs)
    for copy in outs:
        copy.wait()


def last_kernel(
    scales_ref, cov_ref, res_in, sparse_in, low_ref, sparse_out,
    a_ref, x_ref, a3, xl, xr, wl, res_ref, sparse_ref, in_sems, out_sems,
):
    ins = moves(((res_in, res_ref), (sparse_in, sparse_ref)), in_sems)
    put_inverse(cov_ref, scales_ref, a_ref, x_ref, a3, xl, xr, wl)
    for copy in ins:
        copy.wait()
    outs = moves(((sparse_ref, sparse_out),), out_sems)
    low_ref[...] = low_of(res_ref, xl, xr)
    outs[0].wait()


VM = pl.BlockSpec(memory_space=pltpu.VMEM)
SM = pl.BlockSpec(memory_space=pltpu.SMEM)
HBM = pl.BlockSpec(memory_space=pl.ANY)


def inverse_scratch():
    return [
        pltpu.VMEM((NCH, NCH), F32),
        pltpu.VMEM((NCH, NCH), F32),
        pltpu.VMEM((3 * NCH, NCH), BF16),
        pltpu.VMEM((NCH, 3 * NCH), BF16),
        pltpu.VMEM((3 * NCH, NCH), BF16),
        pltpu.VMEM((NCH, 3 * NCH), BF16),
    ]


def middle_stage(scales, cov, res, sky, thr):
    pix = sky.shape[0]
    return pl.pallas_call(
        middle_kernel,
        name="middle_stage",
        out_shape=(
            jax.ShapeDtypeStruct((pix, NCH), F32),
            jax.ShapeDtypeStruct((pix, NCH), F32),
            jax.ShapeDtypeStruct((ROWS, 128), F32),
        ),
        in_specs=[SM, VM, HBM, HBM, VM],
        out_specs=(HBM, HBM, VM),
        scratch_shapes=inverse_scratch()
        + [pltpu.VMEM((pix, NCH), F32)] * 4
        + [pltpu.SemaphoreType.DMA((2,))] * 2
        + reduce_scratch(),
        compiler_params=pltpu.CompilerParams(collective_id=3, has_side_effects=True),
    )(scales, cov, res, sky, thr)


def last_stage(scales, cov, res, sparse):
    return pl.pallas_call(
        last_kernel,
        name="last_stage",
        out_shape=(jax.ShapeDtypeStruct(res.shape, F32), jax.ShapeDtypeStruct(res.shape, F32)),
        in_specs=[SM, VM, HBM, HBM],
        out_specs=(VM, HBM),
        scratch_shapes=inverse_scratch()
        + [pltpu.VMEM(res.shape, F32)] * 2
        + [pltpu.SemaphoreType.DMA((2,)), pltpu.SemaphoreType.DMA((1,))],
    )(scales, cov, res, sparse)


SB = 64
HP = NPIX // 2
WIDE = 2 * X * Z
GROUPS = 2
SUBS = 2


def front_kernel(
    ord_ref, row_ref, leg_hbm, co_hbm, thr_ref, sky_out, res_out, cov_ref, out_ref,
    leg_v, co_v, sp, rb, th, tl, trig_a, trig_b, par, rhs, stage,
    ls, s1, r1, s2, r2, *first_refs,
):
    slots, cycles, degrees = leg_v.shape
    total = WIDE * slots
    gs = slots // GROUPS
    w = lax.axis_index("wide")
    y = lax.axis_index("narrow")
    core = lax.rem(w, 2)
    x = lax.rem(w // 2, X)
    z = w // (2 * X)

    offsets = [(dz, dx, dc) for dz in range(Z) for dx in range(X) for dc in range(2)][1:]
    offsets.sort(key=lambda o: (-min(o[0], Z - o[0]) - min(o[1], X - o[1]), o[1], o[2], o[0]))

    def at(sign, o):
        dz, dx, dc = o
        pz = lax.rem(z + (dz if sign > 0 else Z - dz), Z)
        px = lax.rem(x + (dx if sign > 0 else X - dx), X)
        return pz * 2 * X + px * 2 + (lax.rem(core + dc, 2))

    def ring(d):
        return (w, lax.rem(y + d, Y))

    def loads(s):
        return [pltpu.make_async_copy(leg_hbm.at[s], leg_v.at[s], ls.at[0, s])] + [
            pltpu.make_async_copy(co_hbm.at[k, s], co_v.at[s, :, k * 128 : (k + 1) * 128], ls.at[1 + k, s])
            for k in range(2)
        ]

    pending = [loads(s) for s in range(slots)]
    for copies in pending:
        for copy in copies:
            copy.start()

    barrier = pltpu.get_barrier_semaphore()
    greet()
    for o in offsets:
        pl.semaphore_signal(barrier, inc=1, device_id=(at(1, o), y), device_id_type=MESH)
    for d in range(1, Y):
        pl.semaphore_signal(barrier, inc=1, device_id=ring(d), device_id_type=MESH)

    def remote(src, dst, send, recv, peer):
        return pltpu.make_async_remote_copy(
            src_ref=src, dst_ref=dst, send_sem=send, recv_sem=recv, device_id=peer, device_id_type=MESH
        )

    degree = lax.broadcasted_iota(jnp.int32, (cycles, degrees), 1)
    sends = {}
    for g in range(GROUPS):
        for t in range(gs):
            s = g * gs + t
            for copy in pending[s]:
                copy.wait()
            order = ord_ref[w * slots + s]
            table = jnp.where(degree >= order, leg_v[s].astype(F32), 0.0).astype(BF16)
            value = dot(table, co_v[s])
            for k in range(2):
                sp[g, pl.ds(k * gs + t, cycles, stride=2 * gs), :] = value[:, k * 128 : (k + 1) * 128]
        if g == 0:
            pl.semaphore_wait(barrier, len(offsets) + Y - 1 + GREETED)
        for r, o in enumerate(offsets):
            to = at(1, o)
            sends[g, r] = remote(
                sp.at[g, pl.ds(pl.multiple_of(to * 2 * gs, 8), 2 * gs), :], rb.at[g, w], s1.at[g, r], r1.at[g, r], (to, y)
            )
            sends[g, r].start()

    orders = row_ref[...]
    weights = jnp.where(orders == 0, 1.0, 2.0).astype(F32)

    def trig(ref, steps, stride, weight):
        turn = orders * (lax.broadcasted_iota(jnp.int32, (steps, total), 0) * stride)
        angle = jnp.bitwise_and(turn, NPIX - 1).astype(F32) * (2.0 * math.pi / NPIX)
        ref[0] = weight * jnp.cos(angle)
        ref[1] = weight * jnp.sin(angle)

    trig(trig_a, HP // SB, SB, weights)
    trig(trig_b, SB, 1, 1.0)
    even = (1 - jnp.bitwise_and(orders, 1)).astype(F32)
    for b in range(total // 128):
        par[b * 128 : (b + 1) * 128, :] = jnp.broadcast_to(even[:, b * 128 : (b + 1) * 128], (128, 128)).T

    def fill(a, carry):
        rows = pl.ds(pl.multiple_of(a * SB, SB), SB)
        ca = trig_a[0, pl.ds(a, 1), :]
        sa = trig_a[1, pl.ds(a, 1), :]
        cb, sb = trig_b[0], trig_b[1]
        for k, value in enumerate((ca * cb - sa * sb, -(sa * cb + ca * sb))):
            hi, lo = split(value)
            th[rows, k * total : (k + 1) * total] = hi
            tl[rows, k * total : (k + 1) * total] = lo
        return carry

    lax.fori_loop(0, HP // SB, fill, 0)

    def prepare(src):
        rows = pl.ds(pl.multiple_of(src * slots, slots), slots)
        evens = par[rows, :]
        for k in range(2):
            value = jnp.concatenate([rb[g, src, k * gs : (k + 1) * gs, :] for g in range(GROUPS)], axis=0)
            own = value * evens
            at_k = pl.ds(pl.multiple_of(k * total + src * slots, slots), slots)
            for p, part in enumerate((own, value - own)):
                hi, lo = split(part)
                rhs[at_k, p * 128 : (p + 1) * 128] = hi
                rhs[at_k, 256 + p * 128 : 256 + (p + 1) * 128] = lo

    for g in range(GROUPS):
        rb[g, w] = sp[g, pl.ds(pl.multiple_of(w * 2 * gs, 8), 2 * gs), :]
    prepare(w)
    for r, o in enumerate(offsets):
        for g in range(GROUPS):
            sends[g, r].wait_recv()
        prepare(at(-1, o))

    width = NPIX // Y
    sub = width // SUBS
    outs = {}
    for d in (2, 1):
        first = lax.rem(y + d, Y)
        sign = jnp.where(first < Y // 2, 1.0, -1.0).astype(F32)
        start = lax.rem(first, Y // 2) * width
        for b in range(SUBS):
            rows = pl.ds(pl.multiple_of(start + b * sub, sub), sub)
            top = dot(th[rows, :], rhs[...])
            low = dot(tl[rows, :], rhs[:, 0:256])
            e = top[:, 0:128] + top[:, 256:384] + low[:, 0:128]
            o = sign * (top[:, 128:256] + top[:, 384:512] + low[:, 128:256])
            for q, value in ((d, e + o), ((d + 2) % Y, e - o)):
                mine = slice(b * sub, (b + 1) * sub)
                if q == 0:
                    out_ref[y, mine, :] = value
                else:
                    stage[q - 1, mine, :] = value
                    outs[q, b] = remote(
                        stage.at[q - 1, mine, :], out_ref.at[y, mine, :], s2.at[q, b], r2.at[q, b], ring(q)
                    )
                    outs[q, b].start()
    for copy in outs.values():
        copy.wait_recv()
    first_body(out_ref, thr_ref, sky_out, res_out, cov_ref, *first_refs)
    for copy in outs.values():
        copy.wait_send()
    for copy in sends.values():
        copy.wait_send()


def front_stage(order_table, legendre, coeffs, thr):
    slots, cycles, degrees = legendre.shape
    total = WIDE * slots
    gs = slots // GROUPS
    width = NPIX // Y
    dma = pltpu.SemaphoreType.DMA
    return pl.pallas_call(
        front_kernel,
        name="front_stage",
        out_shape=(
            jax.ShapeDtypeStruct((width, NCH), F32),
            jax.ShapeDtypeStruct((width, NCH), F32),
            jax.ShapeDtypeStruct((ROWS, 128), F32),
        ),
        in_specs=[SM, VM, HBM, HBM, VM],
        out_specs=(HBM, HBM, VM),
        scratch_shapes=[
            pltpu.VMEM((Y, width, 128), F32),
            pltpu.VMEM((slots, cycles, degrees), BF16),
            pltpu.VMEM((slots, degrees, 256), BF16),
            pltpu.VMEM((GROUPS, cycles * 2 * gs, 128), F32),
            pltpu.VMEM((GROUPS, WIDE, 2 * gs, 128), F32),
            pltpu.VMEM((HP, 2 * total), BF16),
            pltpu.VMEM((HP, 2 * total), BF16),
            pltpu.VMEM((2, HP // SB, total), F32),
            pltpu.VMEM((2, SB, total), F32),
            pltpu.VMEM((total, 128), F32),
            pltpu.VMEM((2 * total, 512), BF16),
            pltpu.VMEM((Y - 1, width, 128), F32),
            dma((3, slots)),
            dma((GROUPS, WIDE)),
            dma((GROUPS, WIDE)),
            dma((Y, SUBS)),
            dma((Y, SUBS)),
            pltpu.VMEM((3 * width, NCH), BF16),
            pltpu.VMEM((3 * width, NCH), BF16),
            pltpu.VMEM((width, NCH), F32),
            pltpu.VMEM((width, NCH), F32),
            dma((2,)),
        ]
        + reduce_scratch(),
        compiler_params=pltpu.CompilerParams(collective_id=1, has_side_effects=True),
    )(order_table, order_table[None, :], legendre, coeffs, thr)


def per_device(coeffs, legendre, order_table, thresholds):
    thr = thresholds[None, :]
    scales = jnp.asarray(SCALES + [0.0] * (16 - len(SCALES)), F32)
    sky, res, cov = front_stage(order_table, legendre, coeffs, thr)
    sparse, res, cov = middle_stage(scales, cov, res, sky, thr)
    low, sparse = last_stage(scales, cov, res, sparse)
    return low[None], sparse[None]


def solution(mesh):
    placed = (P(None, "wide", None, "narrow"), P("wide", None, None), P(), P())
    return jax.shard_map(
        per_device,
        mesh=mesh,
        in_specs=placed,
        out_specs=(P("wide", "narrow", None), P("wide", "narrow", None)),
        check_vma=False,
    )
```
